512 devices in a mesh: dp: 32 (over y_lo, z, core), mp: 16 (over x, y_hi).
Axes of the slice: x: 4, y: 8 (y_hi: 4, y_lo: 2; y = y_hi * 2 + y_lo), z: 8, core: 2. Of those that a mesh axis runs over, the one named last changes fastest.
Arguments:
- inputs: bfloat16 [4096, 6144], P('dp', 'mp'), may hold values from -6 to 6
- up_weight: bfloat16 [16, 5, 6, 128, 128], P('mp'), may hold values from -0.25 to 0.25
- up_pick: int32 [16, 5, 6], P('mp'), may hold values from 0 to 2
- down_weight: bfloat16 [16, 5, 3, 2, 128, 128], P('mp'), may hold values from -0.15625 to 0.15625
- down_pick: int32 [16, 5, 3, 2], P('mp'), may hold values from 0 to 5
- cotangent: bfloat16 [4096, 6144], P('dp', 'mp'), may hold values from -6 to 6
Outputs:
- output: bfloat16 [4096, 6144], P('dp', 'mp')
- input_grad: bfloat16 [4096, 6144], P('dp', 'mp')
- up_grad: bfloat16 [16, 5, 6, 128, 128], P('mp')
- down_grad: bfloat16 [16, 5, 3, 2, 128, 128], P('mp')
The draws below stay inside these ranges and needn't reach their ends.
All inputs are finite; a program needn't handle non-finite values.
Results may differ from the reference program's by a relative error of at most 0.005.
Values may be sent and summed in bfloat16 or wider, within the bound.
No kernel may reach another device: no remote copies, remote signals or barrier semaphores. Data moves between devices by JAX's collectives and lax.ppermute only.
A program may use at most 64 MiB of HBM per device.

```python
import math
import jax
import jax.numpy as jnp
import numpy as np
from jax import lax

D = 6144
BLOCK = 128
KD = 2
BITS = 4
LEVELS = 5
DB = 3
HB = 6
TOKENS = 4096
N_MP = 16


def set_ends(drawn, stream_key, smallest, high):
    spot = [jax.random.randint(jax.random.fold_in(stream_key, axis), (), 0, length) for axis, length in enumerate(drawn.shape)]
    main_axis = drawn.shape.index(max(drawn.shape))
    next_to = spot[:main_axis] + [(spot[main_axis] + 1) % drawn.shape[main_axis]] + spot[main_axis + 1:]
    return drawn.at[tuple(spot)].set(smallest).at[tuple(next_to)].set(high)


def level_of(rng, dims, pieces, low, largest):
    level = 1.0
    for axis_at, parts in pieces:
        steps = jax.random.uniform(jax.random.fold_in(jax.random.fold_in(rng, 6), axis_at), (parts,), jnp.float32, low / len(pieces), largest / len(pieces))
        level = level * jnp.repeat(jnp.exp(steps), dims[axis_at] // parts).reshape((-1,) + (1,) * (len(dims) - 1 - axis_at))
    return level


def normal_values(stream_key, extent, deviation, reach, cuts=(), kind=jnp.bfloat16):
    entries = deviation * jax.random.normal(stream_key, extent, jnp.float32)
    if cuts:
        entries = entries * level_of(stream_key, extent, cuts, -0.22, 0.18)
    return jnp.clip(entries, -reach, reach).astype(kind)


def setup_inputs(seed: int = 0) -> dict:
    key_list = jax.random.split(jax.random.key(seed), 7)
    return {
        "inputs": normal_values(key_list[0], (TOKENS, D), 1.0, 6.0, ((0, 32), (1, 16))),
        "up_weight": normal_values(key_list[1], (N_MP, LEVELS, HB, BLOCK, BLOCK), (LEVELS * BLOCK) ** -0.5, 0.25, ((0, 16),)),
        "up_pick": set_ends(jax.random.randint(key_list[2], (N_MP, LEVELS, HB), 0, DB), jax.random.fold_in(key_list[2], 1), 0, DB - 1).astype(jnp.int32),
        "down_weight": normal_values(key_list[3], (N_MP, LEVELS, DB, KD, BLOCK, BLOCK), (LEVELS * KD * BLOCK) ** -0.5, 0.15625, ((0, 16),)),
        "down_pick": set_ends(jax.random.randint(key_list[4], (N_MP, LEVELS, DB, KD), 0, HB), jax.random.fold_in(key_list[4], 1), 0, HB - 1).astype(jnp.int32),
        "cotangent": normal_values(key_list[5], (TOKENS, D), 1.0, 6.0, ((0, 32), (1, 16))),
    }


def partner_ids():
    shard_ids = np.arange(N_MP, dtype=np.int32)[:, None]
    offsets = np.concatenate([np.zeros((1,), np.int32), (2 ** np.arange(BITS)).astype(np.int32)])
    return jnp.asarray((shard_ids ^ offsets[None, :]).astype(np.int32))

def up_map(inputs_f, weights_f, up_pick, partners):
    row_count = inputs_f.shape[0]
    blocks = inputs_f.reshape(row_count, N_MP, DB, BLOCK)
    hidden = jnp.zeros((row_count, N_MP, HB, BLOCK), jnp.float32)
    for level_num in range(LEVELS):
        chosen = blocks[:, partners[:, level_num][:, None], up_pick[:, level_num], :]
        hidden = hidden + jnp.einsum('tsob,sobc->tsoc', chosen, weights_f[:, level_num], precision=lax.Precision.HIGHEST)
    return hidden

def down_map(act_in, weights_f, down_pick, partners):
    row_count = act_in.shape[0]
    blocks = act_in.reshape(row_count, N_MP, HB, BLOCK)
    result = jnp.zeros((row_count, N_MP, DB, BLOCK), jnp.float32)
    for level_num in range(LEVELS):
        for slot_num in range(KD):
            chosen = blocks[:, partners[:, level_num][:, None], down_pick[:, level_num, :, slot_num], :]
            result = result + jnp.einsum('tsob,sobc->tsoc', chosen, weights_f[:, level_num, :, slot_num], precision=lax.Precision.HIGHEST)
    return result

def gelu_tanh(values_in):
    return jax.nn.gelu(values_in, approximate=True)

def reference(inputs, up_weight, up_pick, down_weight, down_pick, cotangent):
    partners = partner_ids()
    up_f = up_weight.astype(jnp.float32)
    down_f = down_weight.astype(jnp.float32)
    block_rows = math.gcd(TOKENS, 1024)
    steps_count = TOKENS // block_rows

    def one_block(running, block_pair):
        inputs_blk, cot_blk = block_pair
        hidden, up_back = jax.vjp(lambda inputs_f, weights_f: up_map(inputs_f, weights_f, up_pick, partners), inputs_blk.astype(jnp.float32), up_f)
        activation = gelu_tanh(hidden).astype(jnp.bfloat16)
        act_f = lax.optimization_barrier(activation).astype(jnp.float32)
        result, down_back = jax.vjp(lambda act_in, weights_f: down_map(act_in, weights_f, down_pick, partners), act_f, down_f)
        act_grad, grad_down = down_back(cot_blk.astype(jnp.float32).reshape(block_rows, N_MP, DB, BLOCK))
        _, gelu_back = jax.vjp(gelu_tanh, hidden)
        hidden_grad = gelu_back(act_grad)[0].astype(jnp.bfloat16)
        hidden_grad_f = lax.optimization_barrier(hidden_grad).astype(jnp.float32)
        grad_inputs, grad_up = up_back(hidden_grad_f)
        out_blk = result.reshape(block_rows, D).astype(jnp.bfloat16)
        return ((running[0] + grad_up, running[1] + grad_down), (out_blk, grad_inputs.astype(jnp.bfloat16)))
    start_sums = (jnp.zeros(up_weight.shape, jnp.float32), jnp.zeros(down_weight.shape, jnp.float32))
    (up_sum, down_sum), (out_all, dx_all) = lax.scan(one_block, start_sums, (inputs.reshape(steps_count, block_rows, D), cotangent.reshape(steps_count, block_rows, D)))
    grad_scale = 1.0 / math.sqrt(TOKENS)
    return (out_all.reshape(TOKENS, D), dx_all.reshape(TOKENS, D), (up_sum * grad_scale).astype(jnp.bfloat16), (down_sum * grad_scale).astype(jnp.bfloat16))
```

```python
import functools
import math

import jax
import jax.numpy as jnp
from jax import lax
from jax.experimental import pallas as pl
from jax.experimental.pallas import tpu as pltpu
from jax.sharding import PartitionSpec as P


F32 = jnp.float32
BF16 = jnp.bfloat16
B = 128
GELU_C = math.sqrt(2.0 / math.pi)
GELU_A = 0.044715


VMEM = pl.BlockSpec(memory_space=pltpu.VMEM)
SMEM = pl.BlockSpec(memory_space=pltpu.SMEM)


def sds(shape, dtype):
    return pltpu.VMEM(shape, dtype)


def call(kernel, outs, in_specs, scratch=()):
    run = pl.pallas_call(
        kernel,
        out_shape=outs,
        in_specs=in_specs,
        out_specs=jax.tree.map(lambda _: VMEM, outs),
        scratch_shapes=list(scratch),
        compiler_params=pltpu.CompilerParams(vmem_limit_bytes=16 << 20),
    )

    def body(*args):
        placed = [
            a if spec is SMEM else pltpu.with_memory_space_constraint(a, pltpu.VMEM)
            for a, spec in zip(args, in_specs)
        ]
        return run(*placed)

    return body


def lanes(index):
    return pl.ds(pl.multiple_of(index * B, B), B)


def dot_nt(a, b):
    return lax.dot_general(a, b, (((1,), (1,)), ((), ())), preferred_element_type=F32)


def dot_tn(a, b):
    return lax.dot_general(a, b, (((0,), (0,)), ((), ())), preferred_element_type=F32)


def back_kernel(levels, db, hb, kd, pick, cot, w, *refs):
    outs, acc = refs[:levels], refs[levels]
    for lvl in range(levels):
        acc[...] = jnp.zeros_like(acc)
        for o in range(db):
            both = jnp.concatenate([w[(lvl * db + o) * kd + k] for k in range(kd)], axis=0)
            term = dot_nt(cot[:, o * B : (o + 1) * B], both)
            for k in range(kd):
                spot = pick[(lvl * db + o) * kd + k]
                acc[spot] += term[:, k * B : (k + 1) * B]
        for h in range(hb):
            outs[lvl][:, h * B : (h + 1) * B] = acc[h].astype(outs[lvl].dtype)


def act_kernel(levels, hb, pick, w, *refs):
    xs, act, slope = refs[:levels], refs[levels], refs[levels + 1]
    for o in range(hb):
        lhs = jnp.concatenate(
            [xs[lvl][:, lanes(pick[lvl * hb + o])] for lvl in range(levels)], axis=1
        )
        rhs = jnp.concatenate([w[lvl * hb + o] for lvl in range(levels)], axis=0)
        v = jnp.dot(lhs, rhs, preferred_element_type=F32)
        sq = v * v
        t = jnp.tanh(GELU_C * (v + GELU_A * (v * sq)))
        half = 0.5 * (1.0 + t)
        act[:, o * B : (o + 1) * B] = (v * half).astype(BF16)
        inner = GELU_C * (1.0 + (3.0 * GELU_A) * sq)
        slope[:, o * B : (o + 1) * B] = half + 0.5 * v * (1.0 - t * t) * inner


def split(core, scr, keep, send):
    half = keep.shape[0]
    keep[...] = scr[pl.ds(core * half, half)]
    send[...] = scr[pl.ds((1 - core) * half, half)].astype(BF16)


def up_kernel(levels, hb, pick, core, slope, *refs):
    back, xs = refs[:levels], refs[levels : 2 * levels]
    hg, keep, send, scr = refs[2 * levels :]
    grad = back[0][...]
    for lvl in range(1, levels):
        grad = grad + back[lvl][...].astype(F32)
    hg[...] = (grad * slope[...]).astype(BF16)
    for o in range(hb):
        right = hg[:, o * B : (o + 1) * B]
        for lvl in range(levels):
            left = xs[lvl][:, lanes(pick[lvl * hb + o])]
            scr[lvl * hb + o] = dot_tn(left, right)
    split(core[0], scr, keep, send)


def in_kernel(levels, db, hb, pick, hg, w, *refs):
    outs, acc = refs[:levels], refs[levels]
    for lvl in range(levels):
        acc[...] = jnp.zeros_like(acc)
        for o in range(hb):
            spot = pick[lvl * hb + o]
            acc[spot] += dot_nt(hg[:, o * B : (o + 1) * B], w[lvl * hb + o])
        for d in range(db):
            outs[lvl][:, d * B : (d + 1) * B] = acc[d].astype(outs[lvl].dtype)


def down_kernel(levels, db, kd, pick, core, cot, *refs):
    acts = refs[:levels]
    keep, send, scr = refs[levels:]
    for o in range(db):
        right = cot[:, o * B : (o + 1) * B]
        for lvl in range(levels):
            for k in range(kd):
                i = (lvl * db + o) * kd + k
                scr[i] = dot_tn(acts[lvl][:, lanes(pick[i])], right)
    split(core[0], scr, keep, send)


def out_kernel(levels, db, kd, pick, w, *refs):
    acts, out = refs[:levels], refs[levels]
    for o in range(db):
        spots = [(lvl * db + o) * kd + k for lvl in range(levels) for k in range(kd)]
        lhs = jnp.concatenate(
            [acts[i // (db * kd)][:, lanes(pick[i])] for i in spots], axis=1
        )
        rhs = jnp.concatenate([w[i] for i in spots], axis=0)
        out[:, o * B : (o + 1) * B] = jnp.dot(lhs, rhs, preferred_element_type=F32).astype(BF16)


def from_partner(block, axis, bit):
    count = lax.axis_size(axis)
    return lax.ppermute(block, axis, [(i, i ^ (1 << bit)) for i in range(count)])


def step(inputs, up_weight, up_pick, down_weight, down_pick, cotangent):
    bits = lax.axis_size("mp").bit_length() - 1
    levels = bits + 1
    tokens = inputs.shape[0]
    db, kd = down_weight.shape[2], down_weight.shape[3]
    hb = up_weight.shape[2]
    dp = lax.axis_size("dp")
    chips = dp // 2
    scale = 1.0 / math.sqrt(tokens * dp)
    n_up, n_down = levels * hb, levels * db * kd
    up_w = up_weight.reshape(n_up, B, B)
    down_w = down_weight.reshape(n_down, B, B)
    up_ids = up_pick.reshape(n_up)
    down_ids = down_pick.reshape(n_down)
    core = lax.rem(lax.axis_index("dp"), 2).reshape(1)
    groups = [[2 * i + c for i in range(chips)] for c in range(2)]

    xs = [inputs] + [from_partner(inputs, "mp", b) for b in range(bits)]

    terms = call(
        functools.partial(back_kernel, levels, db, hb, kd),
        [sds((tokens, hb * B), BF16 if lvl else F32) for lvl in range(levels)],
        [SMEM, VMEM, VMEM],
        [pltpu.VMEM((hb, tokens, B), F32)],
    )(down_ids, cotangent, down_w)
    backs = [terms[0]] + [from_partner(terms[b + 1], "mp", b) for b in range(bits)]

    act, slope = call(
        functools.partial(act_kernel, levels, hb),
        [sds((tokens, hb * B), BF16), sds((tokens, hb * B), F32)],
        [SMEM, VMEM] + [VMEM] * levels,
        (),
    )(up_ids, up_w, *xs)
    acts = [act] + [from_partner(act, "mp", b) for b in range(bits)]

    hg, up_keep, up_send = call(
        functools.partial(up_kernel, levels, hb),
        [
            sds((tokens, hb * B), BF16),
            sds((n_up // 2, B, B), F32),
            sds((n_up // 2, B, B), BF16),
        ],
        [SMEM, SMEM, VMEM] + [VMEM] * (2 * levels),
        [pltpu.VMEM((n_up, B, B), F32)],
    )(up_ids, core, slope, *backs, *xs)

    def exchange(block):
        return lax.all_to_all(
            block, "dp", split_axis=0, concat_axis=0, axis_index_groups=groups, tiled=True
        )

    def reduce_shard(keep, send):
        got = from_partner(send, "dp", 0)
        pair = (keep + got.astype(F32)).astype(BF16)
        parts = exchange(pair.reshape(chips, -1, B))
        return (jnp.sum(parts.astype(F32), axis=0) * scale).astype(BF16)

    def gather(shard):
        wide = lax.optimization_barrier(jnp.broadcast_to(shard[None], (chips,) + shard.shape))
        mine = exchange(wide).reshape(-1, B, B)
        other = from_partner(mine, "dp", 0)
        first = core[0] == 0
        return jnp.concatenate(
            [jnp.where(first, mine, other), jnp.where(first, other, mine)], axis=0
        )

    up_shard = reduce_shard(up_keep, up_send)

    in_terms = call(
        functools.partial(in_kernel, levels, db, hb),
        [sds((tokens, db * B), BF16 if lvl else F32) for lvl in range(levels)],
        [SMEM, VMEM, VMEM],
        [pltpu.VMEM((db, tokens, B), F32)],
    )(up_ids, hg, up_w)
    grad_inputs = in_terms[0]
    for b in range(bits):
        grad_inputs = grad_inputs + from_partner(in_terms[b + 1], "mp", b).astype(F32)

    down_keep, down_send = call(
        functools.partial(down_kernel, levels, db, kd),
        [sds((n_down // 2, B, B), F32), sds((n_down // 2, B, B), BF16)],
        [SMEM, SMEM, VMEM] + [VMEM] * levels,
        [pltpu.VMEM((n_down, B, B), F32)],
    )(down_ids, core, cotangent, *acts)
    down_shard = reduce_shard(down_keep, down_send)

    output = call(
        functools.partial(out_kernel, levels, db, kd),
        sds((tokens, db * B), BF16),
        [SMEM, VMEM] + [VMEM] * levels,
        (),
    )(down_ids, down_w, *acts)

    up_out = gather(up_shard)
    down_out = gather(down_shard)
    return (
        output,
        grad_inputs.astype(BF16),
        up_out.reshape(up_weight.shape),
        down_out.reshape(down_weight.shape),
    )


def solution(mesh):
    placed = (
        P("dp", "mp"),
        P("mp", None, None, None, None),
        P("mp", None, None),
        P("mp", None, None, None, None, None),
        P("mp", None, None, None),
        P("dp", "mp"),
    )
    return jax.shard_map(
        step,
        mesh=mesh,
        in_specs=placed,
        out_specs=(
            P("dp", "mp"),
            P("dp", "mp"),
            P("mp", None, None, None, None),
            P("mp", None, None, None, None, None),
        ),
        check_vma=False,
    )
```

```python
import functools
import math

import jax
import jax.numpy as jnp
from jax import lax
from jax.experimental import pallas as pl
from jax.experimental.pallas import tpu as pltpu
from jax.sharding import PartitionSpec as P


F32 = jnp.float32
BF16 = jnp.bfloat16
B = 128
GELU_C = math.sqrt(2.0 / math.pi)
GELU_A = 0.044715


VMEM = pl.BlockSpec(memory_space=pltpu.VMEM)
SMEM = pl.BlockSpec(memory_space=pltpu.SMEM)


def sds(shape, dtype):
    return pltpu.VMEM(shape, dtype)


def hbm(shape, dtype):
    return jax.ShapeDtypeStruct(shape, dtype)


def call(kernel, outs, in_specs, scratch=()):
    run = pl.pallas_call(
        kernel,
        out_shape=outs,
        in_specs=in_specs,
        out_specs=jax.tree.map(lambda _: VMEM, outs),
        scratch_shapes=list(scratch),
        compiler_params=pltpu.CompilerParams(vmem_limit_bytes=16 << 20),
    )

    def invoke(*args):
        placed = [
            a if spec is SMEM else pltpu.with_memory_space_constraint(a, pltpu.VMEM)
            for a, spec in zip(args, in_specs)
        ]
        return run(*placed)

    return invoke


def lanes(index):
    return pl.ds(pl.multiple_of(index * B, B), B)


def dot_nt(a, b):
    return lax.dot_general(a, b, (((1,), (1,)), ((), ())), preferred_element_type=F32)


def dot_tn(a, b):
    return lax.dot_general(a, b, (((0,), (0,)), ((), ())), preferred_element_type=F32)


def back_kernel(levels, db, hb, kd, pick, cot, w, x, *refs):
    own, sends, acc = refs[0], refs[1:levels], refs[levels]
    wide = db * B
    for send in sends:
        send[:, :wide] = x[...]
    for lvl in range(levels):
        acc[...] = jnp.zeros_like(acc)
        for o in range(db):
            both = jnp.concatenate([w[(lvl * db + o) * kd + k] for k in range(kd)], axis=0)
            term = dot_nt(cot[:, o * B : (o + 1) * B], both)
            for k in range(kd):
                spot = pick[(lvl * db + o) * kd + k]
                acc[spot] += term[:, k * B : (k + 1) * B]
        for h in range(hb):
            if lvl == 0:
                own[:, h * B : (h + 1) * B] = acc[h]
            else:
                sends[lvl - 1][:, wide + h * B : wide + (h + 1) * B] = acc[h].astype(BF16)


def mid_kernel(levels, db, hb, pick, w, x, own, *refs):
    got = refs[: levels - 1]
    in0, hg, sends, acc = refs[levels - 1], refs[levels], refs[levels + 1 : -1], refs[-1]
    xs = (x,) + got
    wide = db * B
    for o in range(hb):
        here = slice(o * B, (o + 1) * B)
        lhs = jnp.concatenate(
            [xs[lvl][:, lanes(pick[lvl * hb + o])] for lvl in range(levels)], axis=1
        )
        rhs = jnp.concatenate([w[lvl * hb + o] for lvl in range(levels)], axis=0)
        v = jnp.dot(lhs, rhs, preferred_element_type=F32)
        sq = v * v
        t = jnp.tanh(GELU_C * (v + GELU_A * (v * sq)))
        half = 0.5 * (1.0 + t)
        act = (v * half).astype(BF16)
        for send in sends:
            send[:, here] = act
        inner = GELU_C * (1.0 + (3.0 * GELU_A) * sq)
        slope = half + 0.5 * v * (1.0 - t * t) * inner
        grad = own[:, here]
        for ref in got:
            grad = grad + ref[:, wide + o * B : wide + (o + 1) * B].astype(F32)
        hg[:, here] = (grad * slope).astype(BF16)
    base = hb * B
    for lvl in range(levels):
        acc[...] = jnp.zeros_like(acc)
        for o in range(hb):
            spot = pick[lvl * hb + o]
            acc[spot] += dot_nt(hg[:, o * B : (o + 1) * B], w[lvl * hb + o])
        for d in range(db):
            if lvl == 0:
                in0[:, d * B : (d + 1) * B] = acc[d]
            else:
                sends[lvl - 1][:, base + d * B : base + (d + 1) * B] = acc[d].astype(BF16)


def split(core, scr, keep, send):
    half = keep.shape[0]
    keep[...] = scr[pl.ds(core * half, half)]
    send[...] = scr[pl.ds((1 - core) * half, half)].astype(BF16)


def up_kernel(levels, hb, pick, core, hg, *refs):
    xs = refs[:levels]
    keep, send, scr = refs[levels:]
    for o in range(hb):
        right = hg[:, o * B : (o + 1) * B]
        for lvl in range(levels):
            left = xs[lvl][:, lanes(pick[lvl * hb + o])]
            scr[lvl * hb + o] = dot_tn(left, right)
    split(core[0], scr, keep, send)


def down_kernel(levels, db, kd, pick, core, cot, *refs):
    acts = refs[:levels]
    keep, send, scr = refs[levels:]
    for o in range(db):
        right = cot[:, o * B : (o + 1) * B]
        for lvl in range(levels):
            for k in range(kd):
                i = (lvl * db + o) * kd + k
                scr[i] = dot_tn(acts[lvl][:, lanes(pick[i])], right)
    split(core[0], scr, keep, send)


def out_kernel(levels, db, hb, kd, pick, w, in0, *refs):
    acts, out, dx = refs[:levels], refs[levels], refs[levels + 1]
    total = in0[...]
    for ref in acts[1:]:
        total = total + ref[:, hb * B :].astype(F32)
    dx[...] = total.astype(BF16)
    for o in range(db):
        spots = [(lvl * db + o) * kd + k for lvl in range(levels) for k in range(kd)]
        lhs = jnp.concatenate(
            [acts[i // (db * kd)][:, lanes(pick[i])] for i in spots], axis=1
        )
        rhs = jnp.concatenate([w[i] for i in spots], axis=0)
        out[:, o * B : (o + 1) * B] = jnp.dot(lhs, rhs, preferred_element_type=F32).astype(BF16)


def shard_kernel(scale, *refs):
    out = refs[-1]
    at = 0
    for ref in refs[:-1]:
        total = ref[0].astype(F32)
        for i in range(1, ref.shape[0]):
            total = total + ref[i].astype(F32)
        total = (total * scale).astype(BF16)
        rows = ref.shape[1]
        for i in range(out.shape[0]):
            out[i, at : at + rows, :] = total
        at += rows


def join_kernel(core, mine, other, *outs):
    at = 0
    for out in outs:
        rows = out.shape[2]
        out[core[0]] = mine[:, at : at + rows, :]
        out[1 - core[0]] = other[:, at : at + rows, :]
        at += rows


def from_partner(block, axis, bit):
    count = lax.axis_size(axis)
    return lax.ppermute(block, axis, [(i, i ^ (1 << bit)) for i in range(count)])


def step(inputs, up_weight, up_pick, down_weight, down_pick, cotangent):
    bits = lax.axis_size("mp").bit_length() - 1
    levels = bits + 1
    tokens = inputs.shape[0]
    db, kd = down_weight.shape[2], down_weight.shape[3]
    hb = up_weight.shape[2]
    dp = lax.axis_size("dp")
    chips = dp // 2
    scale = 1.0 / math.sqrt(tokens * dp)
    n_up, n_down = levels * hb, levels * db * kd
    up_w = up_weight.reshape(n_up, B, B)
    down_w = down_weight.reshape(n_down, B, B)
    up_ids = up_pick.reshape(n_up)
    down_ids = down_pick.reshape(n_down)
    core = lax.rem(lax.axis_index("dp"), 2).reshape(1)
    groups = [[2 * i + c for i in range(chips)] for c in range(2)]

    def over_mp(blocks):
        return [from_partner(blocks[b], "mp", b) for b in reversed(range(bits))][::-1]

    def exchange(block):
        return lax.all_to_all(
            block, "dp", split_axis=0, concat_axis=0, axis_index_groups=groups, tiled=True
        )

    def partials(keep, send):
        got = from_partner(send, "dp", 0)
        pair = (keep + got.astype(F32)).astype(BF16)
        return exchange(pair.reshape(chips, -1, B))

    wide, deep = db * B, hb * B
    own, *first = call(
        functools.partial(back_kernel, levels, db, hb, kd),
        [sds((tokens, deep), F32)] + [sds((tokens, wide + deep), BF16)] * bits,
        [SMEM, VMEM, VMEM, VMEM],
        [pltpu.VMEM((hb, tokens, B), F32)],
    )(down_ids, cotangent, down_w, inputs)
    got = over_mp(first)

    in0, hg, *second = call(
        functools.partial(mid_kernel, levels, db, hb),
        [sds((tokens, wide), F32), sds((tokens, deep), BF16)]
        + [sds((tokens, deep + wide), BF16)] * bits,
        [SMEM] + [VMEM] * (levels + 2),
        [pltpu.VMEM((db, tokens, B), F32)],
    )(up_ids, up_w, inputs, own, *got)
    acts = [second[0]] + over_mp(second)

    def grad_outs(count):
        return [sds((count // 2, B, B), F32), sds((count // 2, B, B), BF16)]

    up_keep, up_send = call(
        functools.partial(up_kernel, levels, hb),
        grad_outs(n_up),
        [SMEM, SMEM, VMEM] + [VMEM] * levels,
        [pltpu.VMEM((n_up, B, B), F32)],
    )(up_ids, core, hg, inputs, *got)
    up_parts = partials(up_keep, up_send)

    down_keep, down_send = call(
        functools.partial(down_kernel, levels, db, kd),
        grad_outs(n_down),
        [SMEM, SMEM, VMEM] + [VMEM] * levels,
        [pltpu.VMEM((n_down, B, B), F32)],
    )(down_ids, core, cotangent, *acts)
    down_parts = partials(down_keep, down_send)

    output, grad_inputs = call(
        functools.partial(out_kernel, levels, db, hb, kd),
        [hbm((tokens, wide), BF16)] * 2,
        [SMEM, VMEM, VMEM] + [VMEM] * levels,
        (),
    )(down_ids, down_w, in0, *acts)

    rows = [up_parts.shape[1], down_parts.shape[1]]
    shard = call(
        functools.partial(shard_kernel, scale), sds((chips, sum(rows), B), BF16), [VMEM, VMEM], ()
    )(up_parts, down_parts)
    mine = exchange(shard)
    other = from_partner(mine, "dp", 0)
    up_out, down_out = call(
        join_kernel, [hbm((2, chips, r, B), BF16) for r in rows], [SMEM, VMEM, VMEM], ()
    )(core, mine, other)
    return (
        output,
        grad_inputs,
        up_out.reshape(up_weight.shape),
        down_out.reshape(down_weight.shape),
    )


def solution(mesh):
    placed = (
        P("dp", "mp"),
        P("mp", None, None, None, None),
        P("mp", None, None),
        P("mp", None, None, None, None, None),
        P("mp", None, None, None),
        P("dp", "mp"),
    )
    return jax.shard_map(
        step,
        mesh=mesh,
        in_specs=placed,
        out_specs=(
            P("dp", "mp"),
            P("dp", "mp"),
            P("mp", None, None, None, None),
            P("mp", None, None, None, None, None),
        ),
        check_vma=False,
    )
```

```python
import functools
import math

import jax
import jax.numpy as jnp
from jax import lax
from jax.experimental import pallas as pl
from jax.experimental.pallas import tpu as pltpu
from jax.sharding import PartitionSpec as P


F32 = jnp.float32
BF16 = jnp.bfloat16
B = 128
GELU_C = math.sqrt(2.0 / math.pi)
GELU_A = 0.044715


VMEM = pl.BlockSpec(memory_space=pltpu.VMEM)
ARG = pl.BlockSpec(memory_space=pltpu.VMEM)
SMEM = pl.BlockSpec(memory_space=pltpu.SMEM)
SPACE = {id(VMEM): pltpu.VMEM, id(ARG): pltpu.HBM}


def sds(shape, dtype):
    return pltpu.VMEM(shape, dtype)


def hbm(shape, dtype):
    return jax.ShapeDtypeStruct(shape, dtype)


def call(kernel, outs, in_specs, scratch=()):
    run = pl.pallas_call(
        kernel,
        out_shape=outs,
        in_specs=in_specs,
        out_specs=jax.tree.map(lambda _: VMEM, outs),
        scratch_shapes=list(scratch),
        compiler_params=pltpu.CompilerParams(vmem_limit_bytes=16 << 20),
    )

    def invoke(*args):
        placed = [
            a if spec is SMEM else pltpu.with_memory_space_constraint(a, SPACE[id(spec)])
            for a, spec in zip(args, in_specs)
        ]
        return run(*placed)

    return invoke


def lanes(index):
    return pl.ds(pl.multiple_of(index * B, B), B)


def dot_nt(a, b):
    return lax.dot_general(a, b, (((1,), (1,)), ((), ())), preferred_element_type=F32)


def dot_tn(a, b):
    return lax.dot_general(a, b, (((0,), (0,)), ((), ())), preferred_element_type=F32)


def back_kernel(levels, db, hb, kd, pick, cot, w, x, *refs):
    own, sends, acc = refs[0], refs[1:levels], refs[levels]
    wide = db * B
    for send in sends:
        send[:, :wide] = x[...]
    for lvl in range(levels):
        acc[...] = jnp.zeros_like(acc)
        for o in range(db):
            both = jnp.concatenate([w[(lvl * db + o) * kd + k] for k in range(kd)], axis=0)
            term = dot_nt(cot[:, o * B : (o + 1) * B], both)
            for k in range(kd):
                spot = pick[(lvl * db + o) * kd + k]
                acc[spot] += term[:, k * B : (k + 1) * B]
        for h in range(hb):
            if lvl == 0:
                own[:, h * B : (h + 1) * B] = acc[h]
            else:
                sends[lvl - 1][:, wide + h * B : wide + (h + 1) * B] = acc[h].astype(BF16)


def mid_kernel(levels, db, hb, pick, w, x, own, *refs):
    got, hg, act = refs[: levels - 1], refs[levels - 1], refs[levels]
    xs = (x,) + got
    wide = db * B
    for o in range(hb):
        here = slice(o * B, (o + 1) * B)
        lhs = jnp.concatenate(
            [xs[lvl][:, lanes(pick[lvl * hb + o])] for lvl in range(levels)], axis=1
        )
        rhs = jnp.concatenate([w[lvl * hb + o] for lvl in range(levels)], axis=0)
        v = jnp.dot(lhs, rhs, preferred_element_type=F32)
        sq = v * v
        t = jnp.tanh(GELU_C * (v + GELU_A * (v * sq)))
        half = 0.5 * (1.0 + t)
        act[:, here] = (v * half).astype(BF16)
        inner = GELU_C * (1.0 + (3.0 * GELU_A) * sq)
        slope = half + 0.5 * v * (1.0 - t * t) * inner
        grad = own[:, here]
        for ref in got:
            grad = grad + ref[:, wide + o * B : wide + (o + 1) * B].astype(F32)
        hg[:, here] = (grad * slope).astype(BF16)


def in_kernel(levels, db, hb, pick, hg, w, *refs):
    outs, acc = refs[:levels], refs[levels]
    for lvl in range(levels):
        acc[...] = jnp.zeros_like(acc)
        for o in range(hb):
            spot = pick[lvl * hb + o]
            acc[spot] += dot_nt(hg[:, o * B : (o + 1) * B], w[lvl * hb + o])
        for d in range(db):
            outs[lvl][:, d * B : (d + 1) * B] = acc[d].astype(outs[lvl].dtype)


def split(core, scr, keep, send):
    half = keep.shape[0]
    keep[...] = scr[pl.ds(core * half, half)]
    send[...] = scr[pl.ds((1 - core) * half, half)].astype(BF16)


def up_kernel(levels, hb, pick, core, hg, *refs):
    xs = refs[:levels]
    keep, send, scr = refs[levels:]
    for o in range(hb):
        right = hg[:, o * B : (o + 1) * B]
        for lvl in range(levels):
            left = xs[lvl][:, lanes(pick[lvl * hb + o])]
            scr[lvl * hb + o] = dot_tn(left, right)
    split(core[0], scr, keep, send)


def down_kernel(levels, db, kd, pick, core, cot, *refs):
    acts = refs[:levels]
    keep, send, scr = refs[levels:]
    for o in range(db):
        right = cot[:, o * B : (o + 1) * B]
        for lvl in range(levels):
            for k in range(kd):
                i = (lvl * db + o) * kd + k
                scr[i] = dot_tn(acts[lvl][:, lanes(pick[i])], right)
    split(core[0], scr, keep, send)


def pair_kernel(*refs):
    out = refs[-1]
    at = 0
    for keep, got in zip(refs[0:-1:2], refs[1:-1:2]):
        rows = keep.shape[1]
        out[:, at : at + rows, :] = (keep[...] + got[...].astype(F32)).astype(BF16)
        at += rows


def dx_kernel(own, *refs):
    total = own[...]
    for ref in refs[:-1]:
        total = total + ref[...].astype(F32)
    refs[-1][...] = total.astype(BF16)


def out_kernel(levels, db, kd, pick, w, *refs):
    acts, out = refs[:levels], refs[levels]
    for o in range(db):
        spots = [(lvl * db + o) * kd + k for lvl in range(levels) for k in range(kd)]
        lhs = jnp.concatenate(
            [acts[i // (db * kd)][:, lanes(pick[i])] for i in spots], axis=1
        )
        rhs = jnp.concatenate([w[i] for i in spots], axis=0)
        out[:, o * B : (o + 1) * B] = jnp.dot(lhs, rhs, preferred_element_type=F32).astype(BF16)


def shard_kernel(scale, parts, out):
    total = parts[0].astype(F32)
    for i in range(1, parts.shape[0]):
        total = total + parts[i].astype(F32)
    total = (total * scale).astype(BF16)
    for i in range(out.shape[0]):
        out[i] = total


def join_kernel(core, mine, other, *outs):
    at = 0
    for out in outs:
        rows = out.shape[2]
        out[core[0]] = mine[:, at : at + rows, :]
        out[1 - core[0]] = other[:, at : at + rows, :]
        at += rows


def from_partner(block, axis, bit):
    count = lax.axis_size(axis)
    return lax.ppermute(block, axis, [(i, i ^ (1 << bit)) for i in range(count)])


def step(inputs, up_weight, up_pick, down_weight, down_pick, cotangent):
    bits = lax.axis_size("mp").bit_length() - 1
    levels = bits + 1
    tokens = inputs.shape[0]
    db, kd = down_weight.shape[2], down_weight.shape[3]
    hb = up_weight.shape[2]
    dp = lax.axis_size("dp")
    chips = dp // 2
    scale = 1.0 / math.sqrt(tokens * dp)
    n_up, n_down = levels * hb, levels * db * kd
    up_w = up_weight.reshape(n_up, B, B)
    down_w = down_weight.reshape(n_down, B, B)
    up_ids = up_pick.reshape(n_up)
    down_ids = down_pick.reshape(n_down)
    core = lax.rem(lax.axis_index("dp"), 2).reshape(1)
    groups = [[2 * i + c for i in range(chips)] for c in range(2)]

    def over_mp(blocks):
        return [from_partner(blocks[b], "mp", b) for b in reversed(range(bits))][::-1]

    def exchange(block):
        return lax.all_to_all(
            block, "dp", split_axis=0, concat_axis=0, axis_index_groups=groups, tiled=True
        )

    wide, deep = db * B, hb * B
    own, *first = call(
        functools.partial(back_kernel, levels, db, hb, kd),
        [sds((tokens, deep), F32)] + [sds((tokens, wide + deep), BF16)] * bits,
        [SMEM, ARG, ARG, ARG],
        [pltpu.VMEM((hb, tokens, B), F32)],
    )(down_ids, cotangent, down_w, inputs)
    got = over_mp(first)

    hg, act = call(
        functools.partial(mid_kernel, levels, db, hb),
        [sds((tokens, deep), BF16)] * 2,
        [SMEM] + [VMEM] * (levels + 2),
        (),
    )(up_ids, up_w, inputs, own, *got)
    acts = [act] + over_mp([act] * bits)

    in0, *in_terms = call(
        functools.partial(in_kernel, levels, db, hb),
        [sds((tokens, wide), F32)] + [sds((tokens, wide), BF16)] * bits,
        [SMEM, VMEM, VMEM],
        [pltpu.VMEM((db, tokens, B), F32)],
    )(up_ids, hg, up_w)
    grad_inputs = call(
        dx_kernel, hbm((tokens, wide), BF16), [VMEM] * levels, ()
    )(in0, *over_mp(in_terms))

    def grad_outs(count):
        return [sds((count // 2, B, B), F32), sds((count // 2, B, B), BF16)]

    up_keep, up_send = call(
        functools.partial(up_kernel, levels, hb),
        grad_outs(n_up),
        [SMEM, SMEM, VMEM] + [VMEM] * levels,
        [pltpu.VMEM((n_up, B, B), F32)],
    )(up_ids, core, hg, inputs, *got)
    up_got = from_partner(up_send, "dp", 0)

    down_keep, down_send = call(
        functools.partial(down_kernel, levels, db, kd),
        grad_outs(n_down),
        [SMEM, SMEM, VMEM] + [VMEM] * levels,
        [pltpu.VMEM((n_down, B, B), F32)],
    )(down_ids, core, cotangent, *acts)
    down_got = from_partner(down_send, "dp", 0)

    output = call(
        functools.partial(out_kernel, levels, db, kd),
        hbm((tokens, wide), BF16),
        [SMEM, VMEM] + [VMEM] * levels,
        (),
    )(down_ids, down_w, *acts)

    halves = [a.reshape(chips, -1, B) for a in (up_keep, up_got, down_keep, down_got)]
    rows = [halves[0].shape[1], halves[2].shape[1]]
    pair = call(pair_kernel, sds((chips, sum(rows), B), BF16), [VMEM] * 4, ())(*halves)
    parts = exchange(pair)
    shard = call(
        functools.partial(shard_kernel, scale), sds((chips, sum(rows), B), BF16), [VMEM], ()
    )(parts)
    mine = exchange(shard)
    other = from_partner(mine, "dp", 0)
    up_out, down_out = call(
        join_kernel, [hbm((2, chips, r, B), BF16) for r in rows], [SMEM, VMEM, VMEM], ()
    )(core, mine, other)
    return (
        output,
        grad_inputs,
        up_out.reshape(up_weight.shape),
        down_out.reshape(down_weight.shape),
    )


def solution(mesh):
    placed = (
        P("dp", "mp"),
        P("mp", None, None, None, None),
        P("mp", None, None),
        P("mp", None, None, None, None, None),
        P("mp", None, None, None),
        P("dp", "mp"),
    )
    return jax.shard_map(
        step,
        mesh=mesh,
        in_specs=placed,
        out_specs=(
            P("dp", "mp"),
            P("dp", "mp"),
            P("mp", None, None, None, None),
            P("mp", None, None, None, None, None),
        ),
        check_vma=False,
    )
```

```python
import functools
import math

import jax
import jax.numpy as jnp
from jax import lax
from jax.experimental import pallas as pl
from jax.experimental.pallas import tpu as pltpu
from jax.sharding import PartitionSpec as P


F32 = jnp.float32
BF16 = jnp.bfloat16
B = 128
GELU_C = math.sqrt(2.0 / math.pi)
GELU_A = 0.044715


VMEM = pl.BlockSpec(memory_space=pltpu.VMEM)
ARG = pl.BlockSpec(memory_space=pltpu.VMEM)
SMEM = pl.BlockSpec(memory_space=pltpu.SMEM)
SPACE = {id(VMEM): pltpu.VMEM, id(ARG): pltpu.HBM}


def sds(shape, dtype):
    return pltpu.VMEM(shape, dtype)


def hbm(shape, dtype):
    return jax.ShapeDtypeStruct(shape, dtype)


def call(kernel, outs, in_specs, scratch=()):
    run = pl.pallas_call(
        kernel,
        out_shape=outs,
        in_specs=in_specs,
        out_specs=jax.tree.map(lambda _: VMEM, outs),
        scratch_shapes=list(scratch),
        compiler_params=pltpu.CompilerParams(vmem_limit_bytes=16 << 20),
    )

    def invoke(*args):
        placed = [
            a if spec is SMEM else pltpu.with_memory_space_constraint(a, SPACE[id(spec)])
            for a, spec in zip(args, in_specs)
        ]
        return run(*placed)

    return invoke


def lanes(index):
    return pl.ds(pl.multiple_of(index * B, B), B)


def dot_nt(a, b):
    return lax.dot_general(a, b, (((1,), (1,)), ((), ())), preferred_element_type=F32)


def dot_tn(a, b):
    return lax.dot_general(a, b, (((0,), (0,)), ((), ())), preferred_element_type=F32)


def back_kernel(levels, db, hb, kd, pick, cot, w, x, *refs):
    own, sends, acc = refs[0], refs[1:levels], refs[levels]
    wide = db * B
    for send in sends:
        send[:, :wide] = x[...]
    for lvl in range(levels):
        acc[...] = jnp.zeros_like(acc)
        for o in range(db):
            both = jnp.concatenate([w[(lvl * db + o) * kd + k] for k in range(kd)], axis=0)
            term = dot_nt(cot[:, o * B : (o + 1) * B], both)
            for k in range(kd):
                spot = pick[(lvl * db + o) * kd + k]
                acc[spot] += term[:, k * B : (k + 1) * B]
        for h in range(hb):
            if lvl == 0:
                own[:, h * B : (h + 1) * B] = acc[h]
            else:
                sends[lvl - 1][:, wide + h * B : wide + (h + 1) * B] = acc[h].astype(BF16)


def mid_kernel(levels, db, hb, pick, w, x, own, *refs):
    got, hg, act = refs[: levels - 1], refs[levels - 1], refs[levels]
    xs = (x,) + got
    wide = db * B
    for o in range(hb):
        here = slice(o * B, (o + 1) * B)
        lhs = jnp.concatenate(
            [xs[lvl][:, lanes(pick[lvl * hb + o])] for lvl in range(levels)], axis=1
        )
        rhs = jnp.concatenate([w[lvl * hb + o] for lvl in range(levels)], axis=0)
        v = jnp.dot(lhs, rhs, preferred_element_type=F32)
        sq = v * v
        t = jnp.tanh(GELU_C * (v + GELU_A * (v * sq)))
        half = 0.5 * (1.0 + t)
        act[:, here] = (v * half).astype(BF16)
        inner = GELU_C * (1.0 + (3.0 * GELU_A) * sq)
        slope = half + 0.5 * v * (1.0 - t * t) * inner
        grad = own[:, here]
        for ref in got:
            grad = grad + ref[:, wide + o * B : wide + (o + 1) * B].astype(F32)
        hg[:, here] = (grad * slope).astype(BF16)


def in_kernel(levels, db, hb, pick, hg, w, *refs):
    outs, acc = refs[:levels], refs[levels]
    for lvl in range(levels):
        acc[...] = jnp.zeros_like(acc)
        for o in range(hb):
            spot = pick[lvl * hb + o]
            acc[spot] += dot_nt(hg[:, o * B : (o + 1) * B], w[lvl * hb + o])
        for d in range(db):
            outs[lvl][:, d * B : (d + 1) * B] = acc[d].astype(outs[lvl].dtype)


def split(core, scr, keep, send):
    half = keep.shape[0]
    keep[...] = scr[pl.ds(core * half, half)]
    send[...] = scr[pl.ds((1 - core) * half, half)].astype(BF16)


def up_kernel(levels, hb, pick, core, hg, *refs):
    xs = refs[:levels]
    keep, send, scr = refs[levels:]
    for o in range(hb):
        right = hg[:, o * B : (o + 1) * B]
        for lvl in range(levels):
            left = xs[lvl][:, lanes(pick[lvl * hb + o])]
            scr[lvl * hb + o] = dot_tn(left, right)
    split(core[0], scr, keep, send)


def down_kernel(levels, db, kd, pick, core, cot, *refs):
    acts = refs[:levels]
    keep, send, scr = refs[levels:]
    for o in range(db):
        right = cot[:, o * B : (o + 1) * B]
        for lvl in range(levels):
            for k in range(kd):
                i = (lvl * db + o) * kd + k
                scr[i] = dot_tn(acts[lvl][:, lanes(pick[i])], right)
    split(core[0], scr, keep, send)


def pair_kernel(*refs):
    out = refs[-1]
    at = 0
    for keep, got in zip(refs[0:-1:2], refs[1:-1:2]):
        rows = keep.shape[1]
        out[:, at : at + rows, :] = (keep[...] + got[...].astype(F32)).astype(BF16)
        at += rows


def dx_kernel(own, *refs):
    total = own[...]
    for ref in refs[:-1]:
        total = total + ref[...].astype(F32)
    refs[-1][...] = total.astype(BF16)


def out_kernel(levels, db, kd, pick, w, *refs):
    acts, out = refs[:levels], refs[levels]
    for o in range(db):
        spots = [(lvl * db + o) * kd + k for lvl in range(levels) for k in range(kd)]
        lhs = jnp.concatenate(
            [acts[i // (db * kd)][:, lanes(pick[i])] for i in spots], axis=1
        )
        rhs = jnp.concatenate([w[i] for i in spots], axis=0)
        out[:, o * B : (o + 1) * B] = jnp.dot(lhs, rhs, preferred_element_type=F32).astype(BF16)


def shard_kernel(scale, parts, out):
    total = parts[0].astype(F32)
    for i in range(1, parts.shape[0]):
        total = total + parts[i].astype(F32)
    total = (total * scale).astype(BF16)
    for i in range(out.shape[0]):
        out[i] = total


def join_kernel(core, mine, other, *outs):
    at = 0
    for out in outs:
        rows = out.shape[2]
        out[core[0]] = mine[:, at : at + rows, :]
        out[1 - core[0]] = other[:, at : at + rows, :]
        at += rows


def from_partner(block, axis, bit):
    count = lax.axis_size(axis)
    return lax.ppermute(block, axis, [(i, i ^ (1 << bit)) for i in range(count)])


def step(inputs, up_weight, up_pick, down_weight, down_pick, cotangent):
    bits = lax.axis_size("mp").bit_length() - 1
    levels = bits + 1
    tokens = inputs.shape[0]
    db, kd = down_weight.shape[2], down_weight.shape[3]
    hb = up_weight.shape[2]
    dp = lax.axis_size("dp")
    chips = dp // 2
    scale = 1.0 / math.sqrt(tokens * dp)
    n_up, n_down = levels * hb, levels * db * kd
    up_w = up_weight.reshape(n_up, B, B)
    down_w = down_weight.reshape(n_down, B, B)
    up_ids = up_pick.reshape(n_up)
    down_ids = down_pick.reshape(n_down)
    core = lax.rem(lax.axis_index("dp"), 2).reshape(1)
    groups = [[2 * i + c for i in range(chips)] for c in range(2)]

    def over_mp(blocks):
        return [from_partner(blocks[b], "mp", b) for b in range(bits)]

    def exchange(block):
        return lax.all_to_all(
            block, "dp", split_axis=0, concat_axis=0, axis_index_groups=groups, tiled=True
        )

    wide, deep = db * B, hb * B
    own, *first = call(
        functools.partial(back_kernel, levels, db, hb, kd),
        [sds((tokens, deep), F32)] + [sds((tokens, wide + deep), BF16)] * bits,
        [SMEM, ARG, ARG, ARG],
        [pltpu.VMEM((hb, tokens, B), F32)],
    )(down_ids, cotangent, down_w, inputs)
    got = over_mp(first)

    hg, act = call(
        functools.partial(mid_kernel, levels, db, hb),
        [sds((tokens, deep), BF16)] * 2,
        [SMEM] + [VMEM] * (levels + 2),
        (),
    )(up_ids, up_w, inputs, own, *got)
    acts = [act] + over_mp([act] * bits)

    in0, *in_terms = call(
        functools.partial(in_kernel, levels, db, hb),
        [sds((tokens, wide), F32)] + [sds((tokens, wide), BF16)] * bits,
        [SMEM, VMEM, VMEM],
        [pltpu.VMEM((db, tokens, B), F32)],
    )(up_ids, hg, up_w)
    grad_inputs = call(
        dx_kernel, hbm((tokens, wide), BF16), [VMEM] * levels, ()
    )(in0, *over_mp(in_terms))

    def grad_outs(count):
        return [sds((count // 2, B, B), F32), sds((count // 2, B, B), BF16)]

    up_keep, up_send = call(
        functools.partial(up_kernel, levels, hb),
        grad_outs(n_up),
        [SMEM, SMEM, VMEM] + [VMEM] * levels,
        [pltpu.VMEM((n_up, B, B), F32)],
    )(up_ids, core, hg, inputs, *got)
    up_got = from_partner(up_send, "dp", 0)

    down_keep, down_send = call(
        functools.partial(down_kernel, levels, db, kd),
        grad_outs(n_down),
        [SMEM, SMEM, VMEM] + [VMEM] * levels,
        [pltpu.VMEM((n_down, B, B), F32)],
    )(down_ids, core, cotangent, *acts)
    down_got = from_partner(down_send, "dp", 0)

    output = call(
        functools.partial(out_kernel, levels, db, kd),
        hbm((tokens, wide), BF16),
        [SMEM, VMEM] + [VMEM] * levels,
        (),
    )(down_ids, down_w, *acts)

    halves = [a.reshape(chips, -1, B) for a in (up_keep, up_got, down_keep, down_got)]
    rows = [halves[0].shape[1], halves[2].shape[1]]
    pair = call(pair_kernel, sds((chips, sum(rows), B), BF16), [VMEM] * 4, ())(*halves)
    parts = exchange(pair)
    shard = call(
        functools.partial(shard_kernel, scale),
        sds((chips, sum(rows), B), BF16),
        [VMEM],
        (),
    )(parts)
    mine = exchange(shard)
    other = from_partner(mine, "dp", 0)
    up_out, down_out = call(
        join_kernel, [hbm((2, chips, r, B), BF16) for r in rows], [SMEM, VMEM, VMEM], ()
    )(core, mine, other)
    return (
        output,
        grad_inputs,
        up_out.reshape(up_weight.shape),
        down_out.reshape(down_weight.shape),
    )


def solution(mesh):
    placed = (
        P("dp", "mp"),
        P("mp", None, None, None, None),
        P("mp", None, None),
        P("mp", None, None, None, None, None),
        P("mp", None, None, None),
        P("dp", "mp"),
    )
    return jax.shard_map(
        step,
        mesh=mesh,
        in_specs=placed,
        out_specs=(
            P("dp", "mp"),
            P("dp", "mp"),
            P("mp", None, None, None, None),
            P("mp", None, None, None, None, None),
        ),
        check_vma=False,
    )
```

```python
import functools
import math

import jax
import jax.numpy as jnp
from jax import lax
from jax.experimental import pallas as pl
from jax.experimental.pallas import tpu as pltpu
from jax.sharding import PartitionSpec as P


F32 = jnp.float32
BF16 = jnp.bfloat16
B = 128
GELU_C = math.sqrt(2.0 / math.pi)
GELU_A = 0.044715


VMEM = pl.BlockSpec(memory_space=pltpu.VMEM)
ARG = pl.BlockSpec(memory_space=pltpu.VMEM)
SMEM = pl.BlockSpec(memory_space=pltpu.SMEM)
SPACE = {id(VMEM): pltpu.VMEM, id(ARG): pltpu.HBM}


def sds(shape, dtype):
    return pltpu.VMEM(shape, dtype)


def hbm(shape, dtype):
    return jax.ShapeDtypeStruct(shape, dtype)


def call(kernel, outs, in_specs, scratch=()):
    run = pl.pallas_call(
        kernel,
        out_shape=outs,
        in_specs=in_specs,
        out_specs=jax.tree.map(lambda _: VMEM, outs),
        scratch_shapes=list(scratch),
        compiler_params=pltpu.CompilerParams(vmem_limit_bytes=16 << 20),
    )

    def invoke(*args):
        placed = [
            a if spec is SMEM else pltpu.with_memory_space_constraint(a, SPACE[id(spec)])
            for a, spec in zip(args, in_specs)
        ]
        return run(*placed)

    return invoke


def lanes(index):
    return pl.ds(pl.multiple_of(index * B, B), B)


def dot_nt(a, b):
    return lax.dot_general(a, b, (((1,), (1,)), ((), ())), preferred_element_type=F32)


def dot_tn(a, b):
    return lax.dot_general(a, b, (((0,), (0,)), ((), ())), preferred_element_type=F32)


def back_kernel(levels, db, hb, kd, pick, cot, w, x, *refs):
    own, sends, acc = refs[0], refs[1:levels], refs[levels]
    wide = db * B
    for send in sends:
        send[:, :wide] = x[...]
    for lvl in range(levels):
        acc[...] = jnp.zeros_like(acc)
        for o in range(db):
            both = jnp.concatenate([w[(lvl * db + o) * kd + k] for k in range(kd)], axis=0)
            term = dot_nt(cot[:, o * B : (o + 1) * B], both)
            for k in range(kd):
                spot = pick[o, k, lvl]
                acc[spot] += term[:, k * B : (k + 1) * B]
        for h in range(hb):
            if lvl == 0:
                own[:, h * B : (h + 1) * B] = acc[h]
            else:
                sends[lvl - 1][:, wide + h * B : wide + (h + 1) * B] = acc[h].astype(BF16)


def mid_kernel(levels, db, hb, pick, w, x, own, *refs):
    got, hg, act = refs[: levels - 1], refs[levels - 1], refs[levels]
    xs = (x,) + got
    wide = db * B
    for o in range(hb):
        here = slice(o * B, (o + 1) * B)
        lhs = jnp.concatenate(
            [xs[lvl][:, lanes(pick[lvl, 0, o])] for lvl in range(levels)], axis=1
        )
        rhs = jnp.concatenate([w[lvl * hb + o] for lvl in range(levels)], axis=0)
        v = jnp.dot(lhs, rhs, preferred_element_type=F32)
        sq = v * v
        t = jnp.tanh(GELU_C * (v + GELU_A * (v * sq)))
        half = 0.5 * (1.0 + t)
        act[:, here] = (v * half).astype(BF16)
        inner = GELU_C * (1.0 + (3.0 * GELU_A) * sq)
        slope = half + 0.5 * v * (1.0 - t * t) * inner
        grad = own[:, here]
        for ref in got:
            grad = grad + ref[:, wide + o * B : wide + (o + 1) * B].astype(F32)
        hg[:, here] = (grad * slope).astype(BF16)


def in_kernel(levels, db, hb, pick, hg, w, *refs):
    outs, acc = refs[:levels], refs[levels]
    for lvl in range(levels):
        acc[...] = jnp.zeros_like(acc)
        for o in range(hb):
            spot = pick[lvl, 0, o]
            acc[spot] += dot_nt(hg[:, o * B : (o + 1) * B], w[lvl * hb + o])
        for d in range(db):
            outs[lvl][:, d * B : (d + 1) * B] = acc[d].astype(outs[lvl].dtype)


def split(core, scr, keep, send):
    half = keep.shape[0]
    keep[...] = scr[pl.ds(core * half, half)]
    send[...] = scr[pl.ds((1 - core) * half, half)].astype(BF16)


def up_kernel(levels, hb, pick, core, hg, *refs):
    xs = refs[:levels]
    keep, send, scr = refs[levels:]
    for o in range(hb):
        right = hg[:, o * B : (o + 1) * B]
        for lvl in range(levels):
            left = xs[lvl][:, lanes(pick[lvl, 0, o])]
            scr[lvl * hb + o] = dot_tn(left, right)
    split(core[0], scr, keep, send)


def down_kernel(levels, db, kd, pick, core, cot, *refs):
    acts = refs[:levels]
    keep, send, scr = refs[levels:]
    for o in range(db):
        right = cot[:, o * B : (o + 1) * B]
        for lvl in range(levels):
            for k in range(kd):
                i = (lvl * db + o) * kd + k
                scr[i] = dot_tn(acts[lvl][:, lanes(pick[o, k, lvl])], right)
    split(core[0], scr, keep, send)


def pair_kernel(keep, got, out):
    out[...] = (keep[...] + got[...].astype(F32)).astype(BF16)


def dx_kernel(own, *refs):
    total = own[...]
    for ref in refs[:-1]:
        total = total + ref[...].astype(F32)
    refs[-1][...] = total.astype(BF16)


def out_kernel(levels, db, kd, pick, w, *refs):
    acts, out = refs[:levels], refs[levels]
    for o in range(db):
        slots = [(lvl, k) for lvl in range(levels) for k in range(kd)]
        lhs = jnp.concatenate(
            [acts[lvl][:, lanes(pick[o, k, lvl])] for lvl, k in slots], axis=1
        )
        rhs = jnp.concatenate([w[(lvl * db + o) * kd + k] for lvl, k in slots], axis=0)
        out[:, o * B : (o + 1) * B] = jnp.dot(lhs, rhs, preferred_element_type=F32).astype(BF16)


def shard_kernel(scale, *refs):
    out = refs[-1]
    at = 0
    for parts in refs[:-1]:
        total = parts[0].astype(F32)
        for i in range(1, parts.shape[0]):
            total = total + parts[i].astype(F32)
        total = (total * scale).astype(BF16)
        rows = parts.shape[1]
        for i in range(out.shape[0]):
            out[i, at : at + rows, :] = total
        at += rows


def join_kernel(core, mine, other, *outs):
    at = 0
    for out in outs:
        rows = out.shape[2]
        out[core[0]] = mine[:, at : at + rows, :]
        out[1 - core[0]] = other[:, at : at + rows, :]
        at += rows


def from_partner(block, axis, bit):
    count = lax.axis_size(axis)
    return lax.ppermute(block, axis, [(i, i ^ (1 << bit)) for i in range(count)])


def step(inputs, up_weight, up_pick, down_weight, down_pick, cotangent):
    bits = lax.axis_size("mp").bit_length() - 1
    levels = bits + 1
    tokens = inputs.shape[0]
    db, kd = down_weight.shape[2], down_weight.shape[3]
    hb = up_weight.shape[2]
    dp = lax.axis_size("dp")
    chips = dp // 2
    scale = 1.0 / math.sqrt(tokens * dp)
    n_up, n_down = levels * hb, levels * db * kd
    up_w = up_weight.reshape(n_up, B, B)
    down_w = down_weight.reshape(n_down, B, B)
    up_ids = up_pick.transpose(1, 0, 2)
    down_ids = down_pick[0].transpose(1, 2, 0)
    core = lax.rem(lax.axis_index("dp"), 2).reshape(1)
    groups = [[2 * i + c for i in range(chips)] for c in range(2)]

    def over_mp(blocks):
        return [from_partner(blocks[b], "mp", b) for b in range(bits)]

    def exchange(block):
        return lax.all_to_all(
            block, "dp", split_axis=0, concat_axis=0, axis_index_groups=groups, tiled=True
        )

    def partials(keep, send):
        got = from_partner(send, "dp", 0)
        pair = call(
            pair_kernel, sds((chips, keep.size // (chips * B), B), BF16), [VMEM] * 2, ()
        )(keep.reshape(chips, -1, B), got.reshape(chips, -1, B))
        return exchange(pair)

    wide, deep = db * B, hb * B
    own, *first = call(
        functools.partial(back_kernel, levels, db, hb, kd),
        [sds((tokens, deep), F32)] + [sds((tokens, wide + deep), BF16)] * bits,
        [SMEM, ARG, ARG, ARG],
        [pltpu.VMEM((hb, tokens, B), F32)],
    )(down_ids, cotangent, down_w, inputs)
    got = over_mp(first)

    hg, act = call(
        functools.partial(mid_kernel, levels, db, hb),
        [sds((tokens, deep), BF16)] * 2,
        [SMEM] + [VMEM] * (levels + 2),
        (),
    )(up_ids, up_w, inputs, own, *got)
    acts = [act] + over_mp([act] * bits)

    in0, *in_terms = call(
        functools.partial(in_kernel, levels, db, hb),
        [sds((tokens, wide), F32)] + [sds((tokens, wide), BF16)] * bits,
        [SMEM, VMEM, VMEM],
        [pltpu.VMEM((db, tokens, B), F32)],
    )(up_ids, hg, up_w)
    grad_inputs = call(
        dx_kernel, hbm((tokens, wide), BF16), [VMEM] * levels, ()
    )(in0, *over_mp(in_terms))

    def grad_outs(count):
        return [sds((count // 2, B, B), F32), sds((count // 2, B, B), BF16)]

    up_keep, up_send = call(
        functools.partial(up_kernel, levels, hb),
        grad_outs(n_up),
        [SMEM, SMEM, VMEM] + [VMEM] * levels,
        [pltpu.VMEM((n_up, B, B), F32)],
    )(up_ids, core, hg, inputs, *got)
    up_parts = partials(up_keep, up_send)

    down_keep, down_send = call(
        functools.partial(down_kernel, levels, db, kd),
        grad_outs(n_down),
        [SMEM, SMEM, VMEM] + [VMEM] * levels,
        [pltpu.VMEM((n_down, B, B), F32)],
    )(down_ids, core, cotangent, *acts)
    down_parts = partials(down_keep, down_send)

    output = call(
        functools.partial(out_kernel, levels, db, kd),
        hbm((tokens, wide), BF16),
        [SMEM, VMEM] + [VMEM] * levels,
        (),
    )(down_ids, down_w, *acts)

    rows = [up_parts.shape[1], down_parts.shape[1]]
    shard = call(
        functools.partial(shard_kernel, scale),
        sds((chips, sum(rows), B), BF16),
        [VMEM] * 2,
        (),
    )(up_parts, down_parts)
    mine = exchange(shard)
    other = from_partner(mine, "dp", 0)
    up_out, down_out = call(
        join_kernel, [hbm((2, chips, r, B), BF16) for r in rows], [SMEM, VMEM, VMEM], ()
    )(core, mine, other)
    return (
        output,
        grad_inputs,
        up_out.reshape(up_weight.shape),
        down_out.reshape(down_weight.shape),
    )


def solution(mesh):
    placed = (
        P("dp", "mp"),
        P("mp", None, None, None, None),
        P("mp", None, None),
        P("mp", None, None, None, None, None),
        P("mp", None, None, None),
        P("dp", "mp"),
    )
    return jax.shard_map(
        step,
        mesh=mesh,
        in_specs=placed,
        out_specs=(
            P("dp", "mp"),
            P("dp", "mp"),
            P("mp", None, None, None, None),
            P("mp", None, None, None, None, None),
        ),
        check_vma=False,
    )
```

```python
import functools
import math

import jax
import jax.numpy as jnp
from jax import lax
from jax.experimental import pallas as pl
from jax.experimental.pallas import tpu as pltpu
from jax.sharding import PartitionSpec as P


F32 = jnp.float32
BF16 = jnp.bfloat16
B = 128
GELU_C = math.sqrt(2.0 / math.pi)
GELU_A = 0.044715


VMEM = pl.BlockSpec(memory_space=pltpu.VMEM)
ARG = pl.BlockSpec(memory_space=pltpu.VMEM)
SMEM = pl.BlockSpec(memory_space=pltpu.SMEM)
SPACE = {id(VMEM): pltpu.VMEM, id(ARG): pltpu.HBM}


def sds(shape, dtype):
    return pltpu.VMEM(shape, dtype)


def hbm(shape, dtype):
    return jax.ShapeDtypeStruct(shape, dtype)


def call(kernel, outs, in_specs, scratch=()):
    run = pl.pallas_call(
        kernel,
        out_shape=outs,
        in_specs=in_specs,
        out_specs=jax.tree.map(lambda _: VMEM, outs),
        scratch_shapes=list(scratch),
        compiler_params=pltpu.CompilerParams(vmem_limit_bytes=16 << 20),
    )

    def invoke(*args):
        placed = [
            a if spec is SMEM else pltpu.with_memory_space_constraint(a, SPACE[id(spec)])
            for a, spec in zip(args, in_specs)
        ]
        return run(*placed)

    return invoke


def lanes(index):
    return pl.ds(pl.multiple_of(index * B, B), B)


def dot_nt(a, b):
    return lax.dot_general(a, b, (((1,), (1,)), ((), ())), preferred_element_type=F32)


def dot_tn(a, b):
    return lax.dot_general(a, b, (((0,), (0,)), ((), ())), preferred_element_type=F32)


def back_kernel(levels, db, hb, kd, pick, cot, w, x, *refs):
    own, sends, acc = refs[0], refs[1:levels], refs[levels]
    wide = db * B
    for send in sends:
        send[:, :wide] = x[...]
    for lvl in range(levels):
        acc[...] = jnp.zeros_like(acc)
        for o in range(db):
            both = jnp.concatenate([w[(lvl * db + o) * kd + k] for k in range(kd)], axis=0)
            term = dot_nt(cot[:, o * B : (o + 1) * B], both)
            for k in range(kd):
                spot = pick[o, k, lvl]
                acc[spot] += term[:, k * B : (k + 1) * B]
        for h in range(hb):
            if lvl == 0:
                own[:, h * B : (h + 1) * B] = acc[h]
            else:
                sends[lvl - 1][:, wide + h * B : wide + (h + 1) * B] = acc[h].astype(BF16)


def mid_kernel(levels, db, hb, pick, w, x, own, *refs):
    got, hg, act = refs[: levels - 1], refs[levels - 1], refs[levels]
    xs = (x,) + got
    wide = db * B
    for o in range(hb):
        here = slice(o * B, (o + 1) * B)
        lhs = jnp.concatenate(
            [xs[lvl][:, lanes(pick[lvl, 0, o])] for lvl in range(levels)], axis=1
        )
        rhs = jnp.concatenate([w[lvl * hb + o] for lvl in range(levels)], axis=0)
        v = jnp.dot(lhs, rhs, preferred_element_type=F32)
        sq = v * v
        t = jnp.tanh(GELU_C * (v + GELU_A * (v * sq)))
        half = 0.5 * (1.0 + t)
        act[:, here] = (v * half).astype(BF16)
        inner = GELU_C * (1.0 + (3.0 * GELU_A) * sq)
        slope = half + 0.5 * v * (1.0 - t * t) * inner
        grad = own[:, here]
        for ref in got:
            grad = grad + ref[:, wide + o * B : wide + (o + 1) * B].astype(F32)
        hg[:, here] = (grad * slope).astype(BF16)


def in_kernel(levels, db, hb, pick, hg, w, *refs):
    outs, acc = refs[:levels], refs[levels]
    for lvl in range(levels):
        acc[...] = jnp.zeros_like(acc)
        for o in range(hb):
            spot = pick[lvl, 0, o]
            acc[spot] += dot_nt(hg[:, o * B : (o + 1) * B], w[lvl * hb + o])
        for d in range(db):
            outs[lvl][:, d * B : (d + 1) * B] = acc[d].astype(outs[lvl].dtype)


def split(core, scr, keep, send):
    half = keep.shape[0]
    keep[...] = scr[pl.ds(core * half, half)]
    send[...] = scr[pl.ds((1 - core) * half, half)].astype(BF16)


def up_kernel(levels, hb, pick, core, hg, *refs):
    xs = refs[:levels]
    keep, send, scr = refs[levels:]
    for o in range(hb):
        right = hg[:, o * B : (o + 1) * B]
        for lvl in range(levels):
            left = xs[lvl][:, lanes(pick[lvl, 0, o])]
            scr[lvl * hb + o] = dot_tn(left, right)
    split(core[0], scr, keep, send)


def down_kernel(levels, db, kd, pick, core, cot, *refs):
    acts = refs[:levels]
    keep, send, scr = refs[levels:]
    for o in range(db):
        right = cot[:, o * B : (o + 1) * B]
        for lvl in range(levels):
            for k in range(kd):
                i = (lvl * db + o) * kd + k
                scr[i] = dot_tn(acts[lvl][:, lanes(pick[o, k, lvl])], right)
    split(core[0], scr, keep, send)


def pair_kernel(row, keep, got, keep_y, send_y):
    mine, other = row[0], 1 - row[0]
    keep_y[...] = keep[mine] + got[mine].astype(F32)
    send_y[...] = (keep[other] + got[other].astype(F32)).astype(BF16)


def column_kernel(*refs):
    out = refs[-1]
    at = 0
    for keep, got in zip(refs[0:-1:2], refs[1:-1:2]):
        rows = keep.shape[1]
        out[:, at : at + rows, :] = (keep[...] + got[...].astype(F32)).astype(BF16)
        at += rows


def dx_kernel(own, *refs):
    total = own[...]
    for ref in refs[:-1]:
        total = total + ref[...].astype(F32)
    refs[-1][...] = total.astype(BF16)


def out_kernel(levels, db, kd, pick, w, *refs):
    acts, out = refs[:levels], refs[levels]
    for o in range(db):
        slots = [(lvl, k) for lvl in range(levels) for k in range(kd)]
        lhs = jnp.concatenate(
            [acts[lvl][:, lanes(pick[o, k, lvl])] for lvl, k in slots], axis=1
        )
        rhs = jnp.concatenate([w[(lvl * db + o) * kd + k] for lvl, k in slots], axis=0)
        out[:, o * B : (o + 1) * B] = jnp.dot(lhs, rhs, preferred_element_type=F32).astype(BF16)


def shard_kernel(scale, parts, out):
    total = parts[0].astype(F32)
    for i in range(1, parts.shape[0]):
        total = total + parts[i].astype(F32)
    total = (total * scale).astype(BF16)
    for i in range(out.shape[0]):
        out[i] = total


def join_kernel(core, mine, other, *outs):
    at = 0
    for out in outs:
        rows = out.shape[2]
        out[core[0]] = mine[:, at : at + rows, :]
        out[1 - core[0]] = other[:, at : at + rows, :]
        at += rows


def from_partner(block, axis, bit):
    count = lax.axis_size(axis)
    return lax.ppermute(block, axis, [(i, i ^ (1 << bit)) for i in range(count)])


def step(inputs, up_weight, up_pick, down_weight, down_pick, cotangent):
    bits = lax.axis_size("mp").bit_length() - 1
    levels = bits + 1
    tokens = inputs.shape[0]
    db, kd = down_weight.shape[2], down_weight.shape[3]
    hb = up_weight.shape[2]
    dp = lax.axis_size("dp")
    chips = dp // 2
    scale = 1.0 / math.sqrt(tokens * dp)
    n_up, n_down = levels * hb, levels * db * kd
    up_w = up_weight.reshape(n_up, B, B)
    down_w = down_weight.reshape(n_down, B, B)
    up_ids = up_pick.transpose(1, 0, 2)
    down_ids = down_pick[0].transpose(1, 2, 0)
    core = lax.rem(lax.axis_index("dp"), 2).reshape(1)
    row = lax.div(lax.axis_index("dp"), chips).reshape(1)
    deep_z = chips // 2
    chip_groups = [[2 * i + c for i in range(chips)] for c in range(2)]
    column_groups = [
        [chips * r + 2 * i + c for i in range(deep_z)] for r in range(2) for c in range(2)
    ]
    row_bit = dp.bit_length() - 2

    def over_mp(blocks):
        return [from_partner(blocks[b], "mp", b) for b in range(bits)]

    def exchange(block, groups):
        return lax.all_to_all(
            block, "dp", split_axis=0, concat_axis=0, axis_index_groups=groups, tiled=True
        )

    def partials(keep, send):
        got = from_partner(send, "dp", 0)
        view = (2, deep_z, -1, B)
        rows = keep.size // (chips * B)
        keep_y, send_y = call(
            pair_kernel,
            [sds((deep_z, rows, B), F32), sds((deep_z, rows, B), BF16)],
            [SMEM, VMEM, VMEM],
            (),
        )(row, keep.reshape(view), got.reshape(view))
        return keep_y, from_partner(send_y, "dp", row_bit)

    wide, deep = db * B, hb * B
    own, *first = call(
        functools.partial(back_kernel, levels, db, hb, kd),
        [sds((tokens, deep), F32)] + [sds((tokens, wide + deep), BF16)] * bits,
        [SMEM, ARG, ARG, ARG],
        [pltpu.VMEM((hb, tokens, B), F32)],
    )(down_ids, cotangent, down_w, inputs)
    got = over_mp(first)

    hg, act = call(
        functools.partial(mid_kernel, levels, db, hb),
        [sds((tokens, deep), BF16)] * 2,
        [SMEM] + [VMEM] * (levels + 2),
        (),
    )(up_ids, up_w, inputs, own, *got)
    acts = [act] + over_mp([act] * bits)

    in0, *in_terms = call(
        functools.partial(in_kernel, levels, db, hb),
        [sds((tokens, wide), F32)] + [sds((tokens, wide), BF16)] * bits,
        [SMEM, VMEM, VMEM],
        [pltpu.VMEM((db, tokens, B), F32)],
    )(up_ids, hg, up_w)
    grad_inputs = call(
        dx_kernel, hbm((tokens, wide), BF16), [VMEM] * levels, ()
    )(in0, *over_mp(in_terms))

    def grad_outs(count):
        return [sds((count // 2, B, B), F32), sds((count // 2, B, B), BF16)]

    up_keep, up_send = call(
        functools.partial(up_kernel, levels, hb),
        grad_outs(n_up),
        [SMEM, SMEM, VMEM] + [VMEM] * levels,
        [pltpu.VMEM((n_up, B, B), F32)],
    )(up_ids, core, hg, inputs, *got)
    up_parts = partials(up_keep, up_send)

    down_keep, down_send = call(
        functools.partial(down_kernel, levels, db, kd),
        grad_outs(n_down),
        [SMEM, SMEM, VMEM] + [VMEM] * levels,
        [pltpu.VMEM((n_down, B, B), F32)],
    )(down_ids, core, cotangent, *acts)
    down_parts = partials(down_keep, down_send)

    output = call(
        functools.partial(out_kernel, levels, db, kd),
        hbm((tokens, wide), BF16),
        [SMEM, VMEM] + [VMEM] * levels,
        (),
    )(down_ids, down_w, *acts)

    rows = [up_parts[0].shape[1], down_parts[0].shape[1]]
    column = call(
        column_kernel, sds((deep_z, sum(rows), B), BF16), [VMEM] * 4, ()
    )(*up_parts, *down_parts)
    parts = exchange(column, column_groups)
    shard = call(
        functools.partial(shard_kernel, scale),
        sds((chips, sum(rows), B), BF16),
        [VMEM],
        (),
    )(parts)
    mine = exchange(shard, chip_groups)
    other = from_partner(mine, "dp", 0)
    up_out, down_out = call(
        join_kernel, [hbm((2, chips, r, B), BF16) for r in rows], [SMEM, VMEM, VMEM], ()
    )(core, mine, other)
    return (
        output,
        grad_inputs,
        up_out.reshape(up_weight.shape),
        down_out.reshape(down_weight.shape),
    )


def solution(mesh):
    placed = (
        P("dp", "mp"),
        P("mp", None, None, None, None),
        P("mp", None, None),
        P("mp", None, None, None, None, None),
        P("mp", None, None, None),
        P("dp", "mp"),
    )
    return jax.shard_map(
        step,
        mesh=mesh,
        in_specs=placed,
        out_specs=(
            P("dp", "mp"),
            P("dp", "mp"),
            P("mp", None, None, None, None),
            P("mp", None, None, None, None, None),
        ),
        check_vma=False,
    )
```

```python
import functools
import math

import jax
import jax.numpy as jnp
from jax import lax
from jax.experimental import pallas as pl
from jax.experimental.pallas import tpu as pltpu
from jax.sharding import PartitionSpec as P


F32 = jnp.float32
BF16 = jnp.bfloat16
B = 128
GELU_C = math.sqrt(2.0 / math.pi)
GELU_A = 0.044715


VMEM = pl.BlockSpec(memory_space=pltpu.VMEM)
ARG = pl.BlockSpec(memory_space=pltpu.VMEM)
SMEM = pl.BlockSpec(memory_space=pltpu.SMEM)
SPACE = {id(VMEM): pltpu.VMEM, id(ARG): pltpu.HBM}


def sds(shape, dtype):
    return pltpu.VMEM(shape, dtype)


def hbm(shape, dtype):
    return jax.ShapeDtypeStruct(shape, dtype)


def call(kernel, outs, in_specs, scratch=()):
    run = pl.pallas_call(
        kernel,
        out_shape=outs,
        in_specs=in_specs,
        out_specs=jax.tree.map(lambda _: VMEM, outs),
        scratch_shapes=list(scratch),
        compiler_params=pltpu.CompilerParams(vmem_limit_bytes=16 << 20),
    )

    def invoke(*args):
        placed = [
            a if spec is SMEM else pltpu.with_memory_space_constraint(a, SPACE[id(spec)])
            for a, spec in zip(args, in_specs)
        ]
        return run(*placed)

    return invoke


def lanes(index):
    return pl.ds(pl.multiple_of(index * B, B), B)


def dot_nt(a, b):
    return lax.dot_general(a, b, (((1,), (1,)), ((), ())), preferred_element_type=F32)


def dot_tn(a, b):
    return lax.dot_general(a, b, (((0,), (0,)), ((), ())), preferred_element_type=F32)


def back_kernel(levels, db, hb, kd, pick, cot, w, x, *refs):
    own, sends, acc = refs[0], refs[1:levels], refs[levels]
    wide = db * B
    for send in sends:
        send[:, :wide] = x[...]
    for lvl in range(levels):
        acc[...] = jnp.zeros_like(acc)
        for o in range(db):
            both = jnp.concatenate([w[(lvl * db + o) * kd + k] for k in range(kd)], axis=0)
            term = dot_nt(cot[:, o * B : (o + 1) * B], both)
            for k in range(kd):
                spot = pick[o, k, lvl]
                acc[spot] += term[:, k * B : (k + 1) * B]
        for h in range(hb):
            if lvl == 0:
                own[:, h * B : (h + 1) * B] = acc[h]
            else:
                sends[lvl - 1][:, wide + h * B : wide + (h + 1) * B] = acc[h].astype(BF16)


def mid_kernel(levels, db, hb, pick, w, x, own, *refs):
    got, hg, act = refs[: levels - 1], refs[levels - 1], refs[levels]
    xs = (x,) + got
    wide = db * B
    for o in range(hb):
        here = slice(o * B, (o + 1) * B)
        lhs = jnp.concatenate(
            [xs[lvl][:, lanes(pick[lvl, 0, o])] for lvl in range(levels)], axis=1
        )
        rhs = jnp.concatenate([w[lvl * hb + o] for lvl in range(levels)], axis=0)
        v = jnp.dot(lhs, rhs, preferred_element_type=F32)
        sq = v * v
        t = jnp.tanh(GELU_C * (v + GELU_A * (v * sq)))
        half = 0.5 * (1.0 + t)
        act[:, here] = (v * half).astype(BF16)
        inner = GELU_C * (1.0 + (3.0 * GELU_A) * sq)
        slope = half + 0.5 * v * (1.0 - t * t) * inner
        grad = own[:, here]
        for ref in got:
            grad = grad + ref[:, wide + o * B : wide + (o + 1) * B].astype(F32)
        hg[:, here] = (grad * slope).astype(BF16)


def in_kernel(levels, db, hb, pick, hg, w, *refs):
    outs, acc = refs[:levels], refs[levels]
    for lvl in range(levels):
        acc[...] = jnp.zeros_like(acc)
        for o in range(hb):
            spot = pick[lvl, 0, o]
            acc[spot] += dot_nt(hg[:, o * B : (o + 1) * B], w[lvl * hb + o])
        for d in range(db):
            outs[lvl][:, d * B : (d + 1) * B] = acc[d].astype(outs[lvl].dtype)


def split(core, scr, keep, send):
    half = keep.shape[0]
    keep[...] = scr[pl.ds(core * half, half)]
    send[...] = scr[pl.ds((1 - core) * half, half)].astype(BF16)


def up_kernel(levels, hb, pick, core, hg, *refs):
    xs = refs[:levels]
    keep, send, scr = refs[levels:]
    for o in range(hb):
        right = hg[:, o * B : (o + 1) * B]
        for lvl in range(levels):
            left = xs[lvl][:, lanes(pick[lvl, 0, o])]
            scr[lvl * hb + o] = dot_tn(left, right)
    split(core[0], scr, keep, send)


def down_kernel(levels, db, kd, pick, core, cot, *refs):
    acts = refs[:levels]
    keep, send, scr = refs[levels:]
    for o in range(db):
        right = cot[:, o * B : (o + 1) * B]
        for lvl in range(levels):
            for k in range(kd):
                i = (lvl * db + o) * kd + k
                scr[i] = dot_tn(acts[lvl][:, lanes(pick[o, k, lvl])], right)
    split(core[0], scr, keep, send)


def pair_kernel(row, keep, got, keep_y, send_y):
    mine, other = row[0], 1 - row[0]
    keep_y[...] = keep[mine] + got[mine].astype(F32)
    send_y[...] = (keep[other] + got[other].astype(F32)).astype(BF16)


def column_kernel(*refs):
    out = refs[-1]
    at = 0
    for keep, got in zip(refs[0:-1:2], refs[1:-1:2]):
        rows = keep.shape[1]
        out[:, at : at + rows, :] = (keep[...] + got[...].astype(F32)).astype(BF16)
        at += rows


def dx_kernel(own, *refs):
    total = own[...]
    for ref in refs[:-1]:
        total = total + ref[...].astype(F32)
    refs[-1][...] = total.astype(BF16)


def out_kernel(levels, db, kd, pick, w, *refs):
    acts, out = refs[:levels], refs[levels]
    for o in range(db):
        slots = [(lvl, k) for lvl in range(levels) for k in range(kd)]
        lhs = jnp.concatenate(
            [acts[lvl][:, lanes(pick[o, k, lvl])] for lvl, k in slots], axis=1
        )
        rhs = jnp.concatenate([w[(lvl * db + o) * kd + k] for lvl, k in slots], axis=0)
        out[:, o * B : (o + 1) * B] = jnp.dot(lhs, rhs, preferred_element_type=F32).astype(BF16)


def shard_kernel(scale, parts, out):
    total = parts[0].astype(F32)
    for i in range(1, parts.shape[0]):
        total = total + parts[i].astype(F32)
    total = (total * scale).astype(BF16)
    for i in range(out.shape[0]):
        out[i] = total


def join_kernel(core, mine, other, *outs):
    at = 0
    for out in outs:
        rows = out.shape[2]
        out[core[0]] = mine[:, at : at + rows, :]
        out[1 - core[0]] = other[:, at : at + rows, :]
        at += rows


def from_partner(block, axis, bit):
    count = lax.axis_size(axis)
    return lax.ppermute(block, axis, [(i, i ^ (1 << bit)) for i in range(count)])


def step(inputs, up_weight, up_pick, down_weight, down_pick, cotangent):
    bits = lax.axis_size("mp").bit_length() - 1
    levels = bits + 1
    tokens = inputs.shape[0]
    db, kd = down_weight.shape[2], down_weight.shape[3]
    hb = up_weight.shape[2]
    dp = lax.axis_size("dp")
    chips = dp // 2
    scale = 1.0 / math.sqrt(tokens * dp)
    n_up, n_down = levels * hb, levels * db * kd
    up_w = up_weight.reshape(n_up, B, B)
    down_w = down_weight.reshape(n_down, B, B)
    up_ids = up_pick.transpose(1, 0, 2)
    down_ids = down_pick[0].transpose(1, 2, 0)
    core = lax.rem(lax.axis_index("dp"), 2).reshape(1)
    row = lax.div(lax.axis_index("dp"), chips).reshape(1)
    deep_z = chips // 2
    turn = sorted(range(deep_z), key=lambda z: f"{z:08b}"[::-1])
    column_groups = {
        (r, c): [chips * r + 2 * ((z + c * deep_z // 2) % deep_z) + c for z in turn]
        for r in range(2)
        for c in range(2)
    }
    chip_groups = [column_groups[0, c] + column_groups[1, c] for c in range(2)]
    column_groups = list(column_groups.values())
    row_bit = dp.bit_length() - 2

    def over_mp(blocks):
        return [from_partner(blocks[b], "mp", b) for b in range(bits)]

    def exchange(block, groups):
        return lax.all_to_all(
            block, "dp", split_axis=0, concat_axis=0, axis_index_groups=groups, tiled=True
        )

    def partials(keep, send):
        got = from_partner(send, "dp", 0)
        view = (2, deep_z, -1, B)
        rows = keep.size // (chips * B)
        keep_y, send_y = call(
            pair_kernel,
            [sds((deep_z, rows, B), F32), sds((deep_z, rows, B), BF16)],
            [SMEM, VMEM, VMEM],
            (),
        )(row, keep.reshape(view), got.reshape(view))
        return keep_y, from_partner(send_y, "dp", row_bit)

    wide, deep = db * B, hb * B
    own, *first = call(
        functools.partial(back_kernel, levels, db, hb, kd),
        [sds((tokens, deep), F32)] + [sds((tokens, wide + deep), BF16)] * bits,
        [SMEM, ARG, ARG, ARG],
        [pltpu.VMEM((hb, tokens, B), F32)],
    )(down_ids, cotangent, down_w, inputs)
    got = over_mp(first)

    hg, act = call(
        functools.partial(mid_kernel, levels, db, hb),
        [sds((tokens, deep), BF16)] * 2,
        [SMEM] + [VMEM] * (levels + 2),
        (),
    )(up_ids, up_w, inputs, own, *got)
    acts = [act] + over_mp([act] * bits)

    in0, *in_terms = call(
        functools.partial(in_kernel, levels, db, hb),
        [sds((tokens, wide), F32)] + [sds((tokens, wide), BF16)] * bits,
        [SMEM, VMEM, VMEM],
        [pltpu.VMEM((db, tokens, B), F32)],
    )(up_ids, hg, up_w)
    grad_inputs = call(
        dx_kernel, hbm((tokens, wide), BF16), [VMEM] * levels, ()
    )(in0, *over_mp(in_terms))

    def grad_outs(count):
        return [sds((count // 2, B, B), F32), sds((count // 2, B, B), BF16)]

    up_keep, up_send = call(
        functools.partial(up_kernel, levels, hb),
        grad_outs(n_up),
        [SMEM, SMEM, VMEM] + [VMEM] * levels,
        [pltpu.VMEM((n_up, B, B), F32)],
    )(up_ids, core, hg, inputs, *got)
    up_parts = partials(up_keep, up_send)

    down_keep, down_send = call(
        functools.partial(down_kernel, levels, db, kd),
        grad_outs(n_down),
        [SMEM, SMEM, VMEM] + [VMEM] * levels,
        [pltpu.VMEM((n_down, B, B), F32)],
    )(down_ids, core, cotangent, *acts)
    down_parts = partials(down_keep, down_send)

    output = call(
        functools.partial(out_kernel, levels, db, kd),
        hbm((tokens, wide), BF16),
        [SMEM, VMEM] + [VMEM] * levels,
        (),
    )(down_ids, down_w, *acts)

    rows = [up_parts[0].shape[1], down_parts[0].shape[1]]
    column = call(
        column_kernel, sds((deep_z, sum(rows), B), BF16), [VMEM] * 4, ()
    )(*up_parts, *down_parts)
    parts = exchange(column, column_groups)
    shard = call(
        functools.partial(shard_kernel, scale),
        sds((chips, sum(rows), B), BF16),
        [VMEM],
        (),
    )(parts)
    mine = exchange(shard, chip_groups)
    other = from_partner(mine, "dp", 0)
    up_out, down_out = call(
        join_kernel, [hbm((2, chips, r, B), BF16) for r in rows], [SMEM, VMEM, VMEM], ()
    )(core, mine, other)
    return (
        output,
        grad_inputs,
        up_out.reshape(up_weight.shape),
        down_out.reshape(down_weight.shape),
    )


def solution(mesh):
    placed = (
        P("dp", "mp"),
        P("mp", None, None, None, None),
        P("mp", None, None),
        P("mp", None, None, None, None, None),
        P("mp", None, None, None),
        P("dp", "mp"),
    )
    return jax.shard_map(
        step,
        mesh=mesh,
        in_specs=placed,
        out_specs=(
            P("dp", "mp"),
            P("dp", "mp"),
            P("mp", None, None, None, None),
            P("mp", None, None, None, None, None),
        ),
        check_vma=False,
    )
```

```python
import functools
import math

import jax
import jax.numpy as jnp
from jax import lax
from jax.experimental import pallas as pl
from jax.experimental.pallas import tpu as pltpu
from jax.sharding import PartitionSpec as P


F32 = jnp.float32
BF16 = jnp.bfloat16
B = 128
GELU_C = math.sqrt(2.0 / math.pi)
GELU_A = 0.044715


VMEM = pl.BlockSpec(memory_space=pltpu.VMEM)
ARG = pl.BlockSpec(memory_space=pltpu.VMEM)
SMEM = pl.BlockSpec(memory_space=pltpu.SMEM)
SPACE = {id(VMEM): pltpu.VMEM, id(ARG): pltpu.HBM}


def sds(shape, dtype):
    return pltpu.VMEM(shape, dtype)


def hbm(shape, dtype):
    return jax.ShapeDtypeStruct(shape, dtype)


def call(kernel, outs, in_specs, scratch=()):
    run = pl.pallas_call(
        kernel,
        out_shape=outs,
        in_specs=in_specs,
        out_specs=jax.tree.map(lambda _: VMEM, outs),
        scratch_shapes=list(scratch),
        compiler_params=pltpu.CompilerParams(vmem_limit_bytes=16 << 20),
    )

    def invoke(*args):
        placed = [
            a if spec is SMEM else pltpu.with_memory_space_constraint(a, SPACE[id(spec)])
            for a, spec in zip(args, in_specs)
        ]
        return run(*placed)

    return invoke


def lanes(index):
    return pl.ds(pl.multiple_of(index * B, B), B)


def dot_nt(a, b):
    return lax.dot_general(a, b, (((1,), (1,)), ((), ())), preferred_element_type=F32)


def dot_tn(a, b):
    return lax.dot_general(a, b, (((0,), (0,)), ((), ())), preferred_element_type=F32)


def back_kernel(levels, db, hb, kd, pick, cot, w, x, *refs):
    own, sends, acc = refs[0], refs[1:levels], refs[levels]
    wide = db * B
    for send in sends:
        send[:, :wide] = x[...]
    for lvl in range(levels):
        acc[...] = jnp.zeros_like(acc)
        for o in range(db):
            both = jnp.concatenate([w[(lvl * db + o) * kd + k] for k in range(kd)], axis=0)
            term = dot_nt(cot[:, o * B : (o + 1) * B], both)
            for k in range(kd):
                spot = pick[o, k, lvl]
                acc[spot] += term[:, k * B : (k + 1) * B]
        for h in range(hb):
            if lvl == 0:
                own[:, h * B : (h + 1) * B] = acc[h]
            else:
                sends[lvl - 1][:, wide + h * B : wide + (h + 1) * B] = acc[h].astype(BF16)


def mid_kernel(levels, db, hb, pick, w, x, own, *refs):
    got, hg, act = refs[: levels - 1], refs[levels - 1], refs[levels]
    xs = (x,) + got
    wide = db * B
    for o in range(hb):
        here = slice(o * B, (o + 1) * B)
        lhs = jnp.concatenate(
            [xs[lvl][:, lanes(pick[lvl, 0, o])] for lvl in range(levels)], axis=1
        )
        rhs = jnp.concatenate([w[lvl * hb + o] for lvl in range(levels)], axis=0)
        v = jnp.dot(lhs, rhs, preferred_element_type=F32)
        sq = v * v
        t = jnp.tanh(GELU_C * (v + GELU_A * (v * sq)))
        half = 0.5 * (1.0 + t)
        act[:, here] = (v * half).astype(BF16)
        inner = GELU_C * (1.0 + (3.0 * GELU_A) * sq)
        slope = half + 0.5 * v * (1.0 - t * t) * inner
        grad = own[:, here]
        for ref in got:
            grad = grad + ref[:, wide + o * B : wide + (o + 1) * B].astype(F32)
        hg[:, here] = (grad * slope).astype(BF16)


def in_kernel(levels, db, hb, pick, hg, w, *refs):
    outs, acc = refs[:levels], refs[levels]
    for lvl in range(levels):
        acc[...] = jnp.zeros_like(acc)
        for o in range(hb):
            spot = pick[lvl, 0, o]
            acc[spot] += dot_nt(hg[:, o * B : (o + 1) * B], w[lvl * hb + o])
        for d in range(db):
            outs[lvl][:, d * B : (d + 1) * B] = acc[d].astype(outs[lvl].dtype)


def split(core, scr, keep, send):
    half = keep.shape[0]
    keep[...] = scr[pl.ds(core * half, half)]
    send[...] = scr[pl.ds((1 - core) * half, half)].astype(BF16)


def up_kernel(levels, hb, pick, core, hg, *refs):
    xs = refs[:levels]
    keep, send, scr = refs[levels:]
    for o in range(hb):
        right = hg[:, o * B : (o + 1) * B]
        for lvl in range(levels):
            left = xs[lvl][:, lanes(pick[lvl, 0, o])]
            scr[lvl * hb + o] = dot_tn(left, right)
    split(core[0], scr, keep, send)


def down_kernel(levels, db, kd, pick, core, cot, *refs):
    acts = refs[:levels]
    keep, send, scr = refs[levels:]
    for o in range(db):
        right = cot[:, o * B : (o + 1) * B]
        for lvl in range(levels):
            for k in range(kd):
                i = (lvl * db + o) * kd + k
                scr[i] = dot_tn(acts[lvl][:, lanes(pick[o, k, lvl])], right)
    split(core[0], scr, keep, send)


def pair_kernel(row, keep, got, keep_y, send_y):
    mine, other = row[0], 1 - row[0]
    keep_y[...] = keep[mine] + got[mine].astype(F32)
    send_y[...] = (keep[other] + got[other].astype(F32)).astype(BF16)


def column_kernel(*refs):
    out = refs[-1]
    at = 0
    for keep, got in zip(refs[0:-1:2], refs[1:-1:2]):
        rows = keep.shape[1]
        out[:, at : at + rows, :] = (keep[...] + got[...].astype(F32)).astype(BF16)
        at += rows


def dx_kernel(own, *refs):
    total = own[...]
    for ref in refs[:-1]:
        total = total + ref[...].astype(F32)
    refs[-1][...] = total.astype(BF16)


def out_kernel(levels, db, kd, pick, w, *refs):
    acts, out = refs[:levels], refs[levels]
    for o in range(db):
        slots = [(lvl, k) for lvl in range(levels) for k in range(kd)]
        lhs = jnp.concatenate(
            [acts[lvl][:, lanes(pick[o, k, lvl])] for lvl, k in slots], axis=1
        )
        rhs = jnp.concatenate([w[(lvl * db + o) * kd + k] for lvl, k in slots], axis=0)
        out[:, o * B : (o + 1) * B] = jnp.dot(lhs, rhs, preferred_element_type=F32).astype(BF16)


def shard_kernel(scale, parts, out):
    total = parts[0].astype(F32)
    for i in range(1, parts.shape[0]):
        total = total + parts[i].astype(F32)
    total = (total * scale).astype(BF16)
    for i in range(out.shape[0]):
        out[i] = total


def join_kernel(places, core, mine, other, *outs):
    for half, source in ((core[0], mine), (1 - core[0], other)):
        for p, (first, second) in enumerate(zip(*places)):
            spot = jnp.where(half == 0, first, second)
            at = 0
            for out in outs:
                rows = out.shape[2]
                out[half, spot] = source[p, at : at + rows, :]
                at += rows


def from_partner(block, axis, bit):
    count = lax.axis_size(axis)
    return lax.ppermute(block, axis, [(i, i ^ (1 << bit)) for i in range(count)])


def step(inputs, up_weight, up_pick, down_weight, down_pick, cotangent):
    bits = lax.axis_size("mp").bit_length() - 1
    levels = bits + 1
    tokens = inputs.shape[0]
    db, kd = down_weight.shape[2], down_weight.shape[3]
    hb = up_weight.shape[2]
    dp = lax.axis_size("dp")
    chips = dp // 2
    scale = 1.0 / math.sqrt(tokens * dp)
    n_up, n_down = levels * hb, levels * db * kd
    up_w = up_weight.reshape(n_up, B, B)
    down_w = down_weight.reshape(n_down, B, B)
    up_ids = up_pick.transpose(1, 0, 2)
    down_ids = down_pick[0].transpose(1, 2, 0)
    core = lax.rem(lax.axis_index("dp"), 2).reshape(1)
    row = lax.div(lax.axis_index("dp"), chips).reshape(1)
    deep_z = chips // 2
    turn = sorted(range(deep_z), key=lambda z: f"{z:08b}"[::-1])
    rings = [[(z + c * deep_z // 2) % deep_z for z in turn] for c in range(2)]
    chip_groups = [[2 * i + c for i in range(chips)] for c in range(2)]
    column_groups = [
        [chips * r + 2 * z + c for z in rings[c]] for r in range(2) for c in range(2)
    ]
    places = [
        [r * deep_z + ring.index(z) for r in range(2) for z in range(deep_z)] for ring in rings
    ]
    row_bit = dp.bit_length() - 2

    def over_mp(blocks):
        return [from_partner(blocks[b], "mp", b) for b in range(bits)]

    def exchange(block, groups):
        return lax.all_to_all(
            block, "dp", split_axis=0, concat_axis=0, axis_index_groups=groups, tiled=True
        )

    def partials(keep, send):
        got = from_partner(send, "dp", 0)
        view = (2, deep_z, -1, B)
        rows = keep.size // (chips * B)
        keep_y, send_y = call(
            pair_kernel,
            [sds((deep_z, rows, B), F32), sds((deep_z, rows, B), BF16)],
            [SMEM, VMEM, VMEM],
            (),
        )(row, keep.reshape(view), got.reshape(view))
        return keep_y, from_partner(send_y, "dp", row_bit)

    wide, deep = db * B, hb * B
    own, *first = call(
        functools.partial(back_kernel, levels, db, hb, kd),
        [sds((tokens, deep), F32)] + [sds((tokens, wide + deep), BF16)] * bits,
        [SMEM, ARG, ARG, ARG],
        [pltpu.VMEM((hb, tokens, B), F32)],
    )(down_ids, cotangent, down_w, inputs)
    got = over_mp(first)

    hg, act = call(
        functools.partial(mid_kernel, levels, db, hb),
        [sds((tokens, deep), BF16)] * 2,
        [SMEM] + [VMEM] * (levels + 2),
        (),
    )(up_ids, up_w, inputs, own, *got)
    acts = [act] + over_mp([act] * bits)

    in0, *in_terms = call(
        functools.partial(in_kernel, levels, db, hb),
        [sds((tokens, wide), F32)] + [sds((tokens, wide), BF16)] * bits,
        [SMEM, VMEM, VMEM],
        [pltpu.VMEM((db, tokens, B), F32)],
    )(up_ids, hg, up_w)
    grad_inputs = call(
        dx_kernel, hbm((tokens, wide), BF16), [VMEM] * levels, ()
    )(in0, *over_mp(in_terms))

    def grad_outs(count):
        return [sds((count // 2, B, B), F32), sds((count // 2, B, B), BF16)]

    up_keep, up_send = call(
        functools.partial(up_kernel, levels, hb),
        grad_outs(n_up),
        [SMEM, SMEM, VMEM] + [VMEM] * levels,
        [pltpu.VMEM((n_up, B, B), F32)],
    )(up_ids, core, hg, inputs, *got)
    up_parts = partials(up_keep, up_send)

    down_keep, down_send = call(
        functools.partial(down_kernel, levels, db, kd),
        grad_outs(n_down),
        [SMEM, SMEM, VMEM] + [VMEM] * levels,
        [pltpu.VMEM((n_down, B, B), F32)],
    )(down_ids, core, cotangent, *acts)
    down_parts = partials(down_keep, down_send)

    output = call(
        functools.partial(out_kernel, levels, db, kd),
        hbm((tokens, wide), BF16),
        [SMEM, VMEM] + [VMEM] * levels,
        (),
    )(down_ids, down_w, *acts)

    rows = [up_parts[0].shape[1], down_parts[0].shape[1]]
    column = call(
        column_kernel, sds((deep_z, sum(rows), B), BF16), [VMEM] * 4, ()
    )(*up_parts, *down_parts)
    parts = exchange(column, column_groups)
    shard = call(
        functools.partial(shard_kernel, scale),
        sds((chips, sum(rows), B), BF16),
        [VMEM],
        (),
    )(parts)
    mine = exchange(shard, chip_groups)
    other = from_partner(mine, "dp", 0)
    up_out, down_out = call(
        functools.partial(join_kernel, places),
        [hbm((2, chips, r, B), BF16) for r in rows],
        [SMEM, VMEM, VMEM],
        (),
    )(core, mine, other)
    return (
        output,
        grad_inputs,
        up_out.reshape(up_weight.shape),
        down_out.reshape(down_weight.shape),
    )


def solution(mesh):
    placed = (
        P("dp", "mp"),
        P("mp", None, None, None, None),
        P("mp", None, None),
        P("mp", None, None, None, None, None),
        P("mp", None, None, None),
        P("dp", "mp"),
    )
    return jax.shard_map(
        step,
        mesh=mesh,
        in_specs=placed,
        out_specs=(
            P("dp", "mp"),
            P("dp", "mp"),
            P("mp", None, None, None, None),
            P("mp", None, None, None, None, None),
        ),
        check_vma=False,
    )
```

```python
import functools
import math

import jax
import jax.numpy as jnp
from jax import lax
from jax.experimental import pallas as pl
from jax.experimental.pallas import tpu as pltpu
from jax.sharding import PartitionSpec as P


F32 = jnp.float32
BF16 = jnp.bfloat16
B = 128
GELU_C = math.sqrt(2.0 / math.pi)
GELU_A = 0.044715


VMEM = pl.BlockSpec(memory_space=pltpu.VMEM)
ARG = pl.BlockSpec(memory_space=pltpu.VMEM)
SMEM = pl.BlockSpec(memory_space=pltpu.SMEM)
SPACE = {id(VMEM): pltpu.VMEM, id(ARG): pltpu.HBM}


def sds(shape, dtype):
    return pltpu.VMEM(shape, dtype)


def hbm(shape, dtype):
    return jax.ShapeDtypeStruct(shape, dtype)


def call(kernel, outs, in_specs, scratch=()):
    run = pl.pallas_call(
        kernel,
        out_shape=outs,
        in_specs=in_specs,
        out_specs=jax.tree.map(lambda _: VMEM, outs),
        scratch_shapes=list(scratch),
        compiler_params=pltpu.CompilerParams(vmem_limit_bytes=16 << 20),
    )

    def invoke(*args):
        placed = [
            a if spec is SMEM else pltpu.with_memory_space_constraint(a, SPACE[id(spec)])
            for a, spec in zip(args, in_specs)
        ]
        return run(*placed)

    return invoke


def lanes(index):
    return pl.ds(pl.multiple_of(index * B, B), B)


def dot_nt(a, b):
    return lax.dot_general(a, b, (((1,), (1,)), ((), ())), preferred_element_type=F32)


def dot_tn(a, b):
    return lax.dot_general(a, b, (((0,), (0,)), ((), ())), preferred_element_type=F32)


def back_kernel(levels, db, hb, kd, early, pick, cot, w, x, *refs):
    own, sends, acc = refs[0], refs[1:levels], refs[levels]
    wide = db * B
    for send in sends[early:]:
        send[:, :wide] = x[...]
    for lvl in range(levels):
        acc[...] = jnp.zeros_like(acc)
        for o in range(db):
            both = jnp.concatenate([w[(lvl * db + o) * kd + k] for k in range(kd)], axis=0)
            term = dot_nt(cot[:, o * B : (o + 1) * B], both)
            for k in range(kd):
                spot = pick[o, k, lvl]
                acc[spot] += term[:, k * B : (k + 1) * B]
        for h in range(hb):
            if lvl == 0:
                own[:, h * B : (h + 1) * B] = acc[h]
            else:
                at = h * B + (wide if lvl > early else 0)
                sends[lvl - 1][:, at : at + B] = acc[h].astype(BF16)


def mid_kernel(levels, db, hb, early, pick, w, *refs):
    xs, own, got = refs[:levels], refs[levels], refs[levels + 1 : 2 * levels]
    hg, act = refs[2 * levels :]
    wide = db * B
    for o in range(hb):
        here = slice(o * B, (o + 1) * B)
        lhs = jnp.concatenate(
            [xs[lvl][:, lanes(pick[lvl, 0, o])] for lvl in range(levels)], axis=1
        )
        rhs = jnp.concatenate([w[lvl * hb + o] for lvl in range(levels)], axis=0)
        v = jnp.dot(lhs, rhs, preferred_element_type=F32)
        sq = v * v
        t = jnp.tanh(GELU_C * (v + GELU_A * (v * sq)))
        half = 0.5 * (1.0 + t)
        act[:, here] = (v * half).astype(BF16)
        inner = GELU_C * (1.0 + (3.0 * GELU_A) * sq)
        slope = half + 0.5 * v * (1.0 - t * t) * inner
        grad = own[:, here]
        for b, ref in enumerate(got):
            at = o * B + (0 if b < early else wide)
            grad = grad + ref[:, at : at + B].astype(F32)
        hg[:, here] = (grad * slope).astype(BF16)


def in_kernel(levels, db, hb, pick, hg, w, *refs):
    outs, acc = refs[:levels], refs[levels]
    for lvl in range(levels):
        acc[...] = jnp.zeros_like(acc)
        for o in range(hb):
            spot = pick[lvl, 0, o]
            acc[spot] += dot_nt(hg[:, o * B : (o + 1) * B], w[lvl * hb + o])
        for d in range(db):
            outs[lvl][:, d * B : (d + 1) * B] = acc[d].astype(outs[lvl].dtype)


def split(core, scr, keep, send):
    half = keep.shape[0]
    keep[...] = scr[pl.ds(core * half, half)]
    send[...] = scr[pl.ds((1 - core) * half, half)].astype(BF16)


def up_kernel(levels, hb, pick, core, hg, *refs):
    xs = refs[:levels]
    keep, send, scr = refs[levels:]
    for o in range(hb):
        right = hg[:, o * B : (o + 1) * B]
        for lvl in range(levels):
            left = xs[lvl][:, lanes(pick[lvl, 0, o])]
            scr[lvl * hb + o] = dot_tn(left, right)
    split(core[0], scr, keep, send)


def down_kernel(levels, db, kd, pick, core, cot, *refs):
    acts = refs[:levels]
    keep, send, scr = refs[levels:]
    for o in range(db):
        right = cot[:, o * B : (o + 1) * B]
        for lvl in range(levels):
            for k in range(kd):
                i = (lvl * db + o) * kd + k
                scr[i] = dot_tn(acts[lvl][:, lanes(pick[o, k, lvl])], right)
    split(core[0], scr, keep, send)


def pair_kernel(row, keep, got, keep_y, send_y):
    mine, other = row[0], 1 - row[0]
    keep_y[...] = keep[mine] + got[mine].astype(F32)
    send_y[...] = (keep[other] + got[other].astype(F32)).astype(BF16)


def column_kernel(*refs):
    out = refs[-1]
    at = 0
    for keep, got in zip(refs[0:-1:2], refs[1:-1:2]):
        rows = keep.shape[1]
        out[:, at : at + rows, :] = (keep[...] + got[...].astype(F32)).astype(BF16)
        at += rows


def dx_kernel(own, *refs):
    total = own[...]
    for ref in refs[:-1]:
        total = total + ref[...].astype(F32)
    refs[-1][...] = total.astype(BF16)


def out_kernel(levels, db, kd, pick, w, *refs):
    acts, out = refs[:levels], refs[levels]
    for o in range(db):
        slots = [(lvl, k) for lvl in range(levels) for k in range(kd)]
        lhs = jnp.concatenate(
            [acts[lvl][:, lanes(pick[o, k, lvl])] for lvl, k in slots], axis=1
        )
        rhs = jnp.concatenate([w[(lvl * db + o) * kd + k] for lvl, k in slots], axis=0)
        out[:, o * B : (o + 1) * B] = jnp.dot(lhs, rhs, preferred_element_type=F32).astype(BF16)


def shard_kernel(scale, parts, out):
    total = parts[0].astype(F32)
    for i in range(1, parts.shape[0]):
        total = total + parts[i].astype(F32)
    total = (total * scale).astype(BF16)
    for i in range(out.shape[0]):
        out[i] = total


def join_kernel(places, core, mine, other, *outs):
    for half, source in ((core[0], mine), (1 - core[0], other)):
        for p, (first, second) in enumerate(zip(*places)):
            spot = jnp.where(half == 0, first, second)
            at = 0
            for out in outs:
                rows = out.shape[2]
                out[half, spot] = source[p, at : at + rows, :]
                at += rows


def from_partner(block, axis, bit):
    count = lax.axis_size(axis)
    return lax.ppermute(block, axis, [(i, i ^ (1 << bit)) for i in range(count)])


def step(inputs, up_weight, up_pick, down_weight, down_pick, cotangent):
    bits = lax.axis_size("mp").bit_length() - 1
    levels = bits + 1
    tokens = inputs.shape[0]
    db, kd = down_weight.shape[2], down_weight.shape[3]
    hb = up_weight.shape[2]
    dp = lax.axis_size("dp")
    chips = dp // 2
    scale = 1.0 / math.sqrt(tokens * dp)
    n_up, n_down = levels * hb, levels * db * kd
    up_w = up_weight.reshape(n_up, B, B)
    down_w = down_weight.reshape(n_down, B, B)
    up_ids = up_pick.transpose(1, 0, 2)
    down_ids = down_pick[0].transpose(1, 2, 0)
    core = lax.rem(lax.axis_index("dp"), 2).reshape(1)
    row = lax.div(lax.axis_index("dp"), chips).reshape(1)
    deep_z = chips // 2
    turn = sorted(range(deep_z), key=lambda z: f"{z:08b}"[::-1])
    rings = [[(z + c * deep_z // 2) % deep_z for z in turn] for c in range(2)]
    chip_groups = [[2 * i + c for i in range(chips)] for c in range(2)]
    column_groups = [
        [chips * r + 2 * z + c for z in rings[c]] for r in range(2) for c in range(2)
    ]
    places = [
        [r * deep_z + ring.index(z) for r in range(2) for z in range(deep_z)] for ring in rings
    ]
    row_bit = dp.bit_length() - 2

    def over_mp(blocks):
        return [from_partner(blocks[b], "mp", b) for b in range(len(blocks))]

    def exchange(block, groups):
        return lax.all_to_all(
            block, "dp", split_axis=0, concat_axis=0, axis_index_groups=groups, tiled=True
        )

    def partials(keep, send):
        got = from_partner(send, "dp", 0)
        view = (2, deep_z, -1, B)
        rows = keep.size // (chips * B)
        keep_y, send_y = call(
            pair_kernel,
            [sds((deep_z, rows, B), F32), sds((deep_z, rows, B), BF16)],
            [SMEM, VMEM, VMEM],
            (),
        )(row, keep.reshape(view), got.reshape(view))
        return keep_y, from_partner(send_y, "dp", row_bit)

    wide, deep = db * B, hb * B
    early = bits // 2
    xs = [inputs] + over_mp([inputs] * early)
    own, *first = call(
        functools.partial(back_kernel, levels, db, hb, kd, early),
        [sds((tokens, deep), F32)]
        + [sds((tokens, deep), BF16)] * early
        + [sds((tokens, wide + deep), BF16)] * (bits - early),
        [SMEM, ARG, ARG, ARG],
        [pltpu.VMEM((hb, tokens, B), F32)],
    )(down_ids, cotangent, down_w, inputs)
    got = over_mp(first)
    xs = xs + got[early:]

    hg, act = call(
        functools.partial(mid_kernel, levels, db, hb, early),
        [sds((tokens, deep), BF16)] * 2,
        [SMEM] + [VMEM] * (2 * levels + 1),
        (),
    )(up_ids, up_w, *xs, own, *got)
    acts = [act] + over_mp([act] * bits)

    in0, *in_terms = call(
        functools.partial(in_kernel, levels, db, hb),
        [sds((tokens, wide), F32)] + [sds((tokens, wide), BF16)] * bits,
        [SMEM, VMEM, VMEM],
        [pltpu.VMEM((db, tokens, B), F32)],
    )(up_ids, hg, up_w)
    grad_inputs = call(
        dx_kernel, hbm((tokens, wide), BF16), [VMEM] * levels, ()
    )(in0, *over_mp(in_terms))

    def grad_outs(count):
        return [sds((count // 2, B, B), F32), sds((count // 2, B, B), BF16)]

    up_keep, up_send = call(
        functools.partial(up_kernel, levels, hb),
        grad_outs(n_up),
        [SMEM, SMEM, VMEM] + [VMEM] * levels,
        [pltpu.VMEM((n_up, B, B), F32)],
    )(up_ids, core, hg, *xs)
    up_parts = partials(up_keep, up_send)

    down_keep, down_send = call(
        functools.partial(down_kernel, levels, db, kd),
        grad_outs(n_down),
        [SMEM, SMEM, VMEM] + [VMEM] * levels,
        [pltpu.VMEM((n_down, B, B), F32)],
    )(down_ids, core, cotangent, *acts)
    down_parts = partials(down_keep, down_send)

    output = call(
        functools.partial(out_kernel, levels, db, kd),
        hbm((tokens, wide), BF16),
        [SMEM, VMEM] + [VMEM] * levels,
        (),
    )(down_ids, down_w, *acts)

    rows = [up_parts[0].shape[1], down_parts[0].shape[1]]
    column = call(
        column_kernel, sds((deep_z, sum(rows), B), BF16), [VMEM] * 4, ()
    )(*up_parts, *down_parts)
    parts = exchange(column, column_groups)
    shard = call(
        functools.partial(shard_kernel, scale),
        sds((chips, sum(rows), B), BF16),
        [VMEM],
        (),
    )(parts)
    mine = exchange(shard, chip_groups)
    other = from_partner(mine, "dp", 0)
    up_out, down_out = call(
        functools.partial(join_kernel, places),
        [hbm((2, chips, r, B), BF16) for r in rows],
        [SMEM, VMEM, VMEM],
        (),
    )(core, mine, other)
    return (
        output,
        grad_inputs,
        up_out.reshape(up_weight.shape),
        down_out.reshape(down_weight.shape),
    )


def solution(mesh):
    placed = (
        P("dp", "mp"),
        P("mp", None, None, None, None),
        P("mp", None, None),
        P("mp", None, None, None, None, None),
        P("mp", None, None, None),
        P("dp", "mp"),
    )
    return jax.shard_map(
        step,
        mesh=mesh,
        in_specs=placed,
        out_specs=(
            P("dp", "mp"),
            P("dp", "mp"),
            P("mp", None, None, None, None),
            P("mp", None, None, None, None, None),
        ),
        check_vma=False,
    )
```
